512 devices in a mesh: cell: 32 (over y_hi, z, core), gene: 16 (over y_lo, x).
Axes of the slice: x: 4, y: 8 (y_hi: 2, y_lo: 4; y = y_hi * 4 + y_lo), z: 8, core: 2. Of those that a mesh axis runs over, the one named last changes fastest.
Arguments:
- counts: int32 [8192, 16384], P('cell', 'gene'), may hold values from 0 to 54, as said below
- cell_totals: int32 [8192], P('cell'), may hold values from 32768 to 294912, as said below
- gene_totals: int32 [16384], P('gene'), may hold values from 997 to 2991, as said below
- test_matrix: bfloat16 [16384, 96], P('gene', 'cell'), may hold values from -0.046875 to 0.046875
Outputs:
- sketch: bfloat16 [8192, 96], P('cell')
- gene_panel: bfloat16 [16384, 96], P('gene')
The draws below stay inside these ranges and needn't reach their ends.
Inputs may be any that keep to these rules, and one draw needn't show every extreme that they name: counts are nonnegative. `cell_totals`: cell totals are positive. `gene_totals`: gene totals are positive.
All inputs are finite; a program needn't handle non-finite values.
Results may differ from the reference program's by a relative error of at most 0.03.
Values may be sent and summed in bfloat16 or wider, within the bound.
No kernel may reach another device: no remote copies, remote signals or barrier semaphores. Data moves between devices by JAX's collectives and lax.ppermute only.
A program may use at most 64 MiB of HBM per device.

```python
import math
import jax
import jax.numpy as jnp
from jax import lax

GENES = 16384
SKETCH = 96
ITERS = 3
CELL_DEV = 256
CELLS = 8192
N_CELL = 32
N_GENE = 16


def levels(key):
    gene_key = jax.random.fold_in(key, 11)
    cell_key = jax.random.fold_in(key, 12)
    gene_level = jax.random.randint(gene_key, (GENES,), 1, 4).astype(jnp.int32)
    gene_level = gene_level.at[0].set(1).at[1].set(3)
    rows = jnp.arange(CELLS, dtype=jnp.int32)
    extra = jax.random.randint(cell_key, (CELLS,), 0, 2).astype(jnp.int32)
    extra = extra.at[0].set(0).at[CELLS - 1].set(1)
    cell_level = 1 + 8 * rows // CELLS + extra
    return (gene_level, cell_level)


def draw_counts(key, part):
    gene_level, cell_level = levels(key)
    span = 2 * cell_level[:, None] * gene_level[None, :] + 1
    raw = jax.random.randint(jax.random.fold_in(key, 13), (CELLS, GENES), 0, 1048576).astype(jnp.int32)
    values = (raw % span).astype(jnp.int32)
    values = values.at[0, 0].set(0)
    values = values.at[CELLS - 1, 1].set(span[CELLS - 1, 1] - 1)
    return values.astype(jnp.int32)


def draw_cell_totals(key, part):
    gene_level, cell_level = levels(key)
    return (cell_level * 2 * GENES).astype(jnp.int32)


def draw_gene_totals(key, part):
    gene_level, cell_level = levels(key)
    return (gene_level * 997).astype(jnp.int32)


def block_scale(rng, shape, shards, low, top_value):
    loudness = 1.0
    for position, blocks in shards:
        steps = jax.random.uniform(jax.random.fold_in(jax.random.fold_in(rng, 6), position), (blocks,), jnp.float32, low / len(shards), top_value / len(shards))
        loudness = loudness * jnp.repeat(jnp.exp(steps), shape[position] // blocks).reshape((-1,) + (1,) * (len(shape) - 1 - position))
    return loudness


def normal_values(own_key, dims, width, bound, split=(), kind=jnp.bfloat16):
    level = block_scale(own_key, dims, split, -0.22, 0.18) if split else 1.0
    values = jax.random.normal(own_key, dims, jnp.float32) * width * level
    return jnp.minimum(jnp.maximum(values, -bound), bound).astype(kind)


def setup_inputs(seed: int = 0) -> dict:
    splits = jax.random.split(jax.random.key(seed), 5)
    counts = draw_counts(jax.random.fold_in(splits[4], 71), 0)
    cell_totals = draw_cell_totals(jax.random.fold_in(splits[4], 71), 0)
    gene_totals = draw_gene_totals(jax.random.fold_in(splits[4], 71), 0)
    test_matrix = normal_values(splits[3], (GENES, SKETCH), GENES ** -0.5, 0.046875, ((0, 16), (1, 32)))
    return dict(counts=counts, cell_totals=cell_totals, gene_totals=gene_totals, test_matrix=test_matrix)


def pearson(counts, cell_totals, fraction):
    expected = cell_totals.astype(jnp.float32)[:, None] * fraction[None, :]
    spread = jnp.sqrt(expected + expected * expected / 100.0)
    return ((counts.astype(jnp.float32) - expected) / spread).astype(jnp.bfloat16)

def rounded(value):
    return lax.optimization_barrier(value.astype(jnp.bfloat16)).astype(jnp.float32)

def reference(counts, cell_totals, gene_totals, test_matrix):
    total = jnp.sum(gene_totals).astype(jnp.int32)
    fraction = gene_totals.astype(jnp.float32) / total.astype(jnp.float32)
    scale = 1.0 / math.sqrt(CELLS + GENES)
    gene_cols = GENES // N_GENE
    count_blocks = counts.reshape(N_CELL, CELL_DEV, GENES)
    total_blocks = cell_totals.reshape(N_CELL, CELL_DEV)

    def cell_side(panel, factor):
        panel_parts = panel.astype(jnp.float32).reshape(N_GENE, gene_cols, SKETCH)

        def one_block(pair):
            rows, totals = pair
            resid = pearson(rows, totals, fraction).astype(jnp.float32).reshape(CELL_DEV, N_GENE, gene_cols)
            parts = jnp.einsum('bjg,jgs->jbs', resid, panel_parts, precision=lax.Precision.HIGHEST)
            return (lax.optimization_barrier(jnp.sum(rounded(parts), axis=0)) * factor).astype(jnp.bfloat16)
        return lax.map(one_block, (count_blocks, total_blocks)).reshape(CELLS, SKETCH)

    def gene_side(sketch):
        sketch_blocks = sketch.reshape(N_CELL, CELL_DEV, SKETCH)

        def add_block(accum, triple):
            rows, totals, part = triple
            resid = pearson(rows, totals, fraction)
            term = lax.dot_general(resid, part, (((0,), (0,)), ((), ())), preferred_element_type=jnp.float32)
            return (accum + rounded(term), None)
        start = jnp.zeros((GENES, SKETCH), jnp.float32)
        accum, unused = lax.scan(add_block, start, (count_blocks, total_blocks, sketch_blocks))
        return (accum * scale).astype(jnp.bfloat16)
    sketch = cell_side(test_matrix, 1.0)
    for step in range(ITERS):
        panel = gene_side(sketch)
        sketch = cell_side(panel, scale)
    gene_panel = gene_side(sketch)
    return (sketch, gene_panel)
```

```python
import math

import jax
import jax.numpy as jnp
import numpy as np
from jax import lax
from jax.sharding import Mesh, PartitionSpec as P

ITERS = 3
Y_HI, Z, CORE, Y_LO, X = 2, 8, 2, 4, 4
F32, BF16 = jnp.float32, jnp.bfloat16


def spread(x, axis, n):
    return lax.all_to_all(jnp.broadcast_to(x[None], (n,) + x.shape), axis, 0, 0, tiled=True)


def gather_sum(x, axis, n, factor=None):
    total = jnp.sum(spread(x, axis, n).astype(F32), axis=0)
    if factor is not None:
        total = total * factor
    return total.astype(BF16)


def shards(counts, cell_totals, gene_totals, test_matrix):
    rows, cols = counts.shape
    scale = 1.0 / math.sqrt(rows * Y_HI * Z * CORE + cols * Y_LO * X)

    swap = [(0, 1), (1, 0)]
    mine = counts.astype(BF16)
    other = lax.ppermute(mine, "y_hi", swap)
    hi = lax.axis_index("y_hi")

    totals = lax.all_to_all(
        jnp.broadcast_to(jnp.sum(gene_totals)[None, None], (Y_LO * X, 1)), ("y_lo", "x"), 0, 0, tiled=True
    )
    total = jnp.sum(totals)
    fraction = gene_totals.astype(F32) / total.astype(F32)
    test = spread(test_matrix.T, "z", Z).reshape(Z * test_matrix.shape[1], cols)
    both_totals = lax.all_gather(lax.all_gather(cell_totals, "core"), "y_hi")

    def resid(block, totals):
        expected = totals.astype(F32)[:, None] * fraction[None, :]
        return (
            (block.astype(F32) - expected) / jnp.sqrt(expected + expected * expected / 100.0)
        ).astype(BF16)

    core = lax.axis_index("core")
    low = jnp.where(hi == 0, mine, other)
    high = jnp.where(hi == 0, other, mine)
    pair = jnp.stack([resid(low, both_totals[0, core]), resid(high, both_totals[1, core])])
    stored = lax.all_to_all(
        jnp.broadcast_to(pair[None], (CORE,) + pair.shape), "core", 0, 0, tiled=True
    )
    stored = stored.reshape(CORE * Y_HI * rows, cols)

    def cell_side(panel, factor):
        part = lax.dot_general(
            panel, stored, (((1,), (1,)), ((), ())), preferred_element_type=F32
        ).astype(BF16)
        return gather_sum(gather_sum(part, "x", X), "y_lo", Y_LO, factor)

    def gene_side(sketch):
        part = jnp.dot(sketch, stored, preferred_element_type=F32).astype(BF16)
        return gather_sum(part, "z", Z, scale)

    sketch = cell_side(test, 1.0)
    for step in range(ITERS):
        panel = gene_side(sketch)
        sketch = cell_side(panel, scale)
    gene_panel = gene_side(sketch)

    width = sketch.shape[0]
    parts = sketch.reshape(width, CORE * Y_HI, rows).transpose(1, 0, 2)
    send = jnp.concatenate(
        [parts, jnp.broadcast_to(gene_panel[None], (CORE * Y_HI, width, cols))], axis=2
    )
    got = lax.all_to_all(send, ("core", "y_hi"), 0, 0, tiled=True)
    got = got.reshape(CORE, Y_HI, Z, width // Z, rows + cols).transpose(1, 2, 0, 3, 4)
    got = got.reshape(CORE * Y_HI * width, rows + cols)
    return (got[:, :rows].T, got[:, rows:].T)


def solution(mesh):
    fine = Mesh(
        np.asarray(mesh.devices).reshape(Y_HI, Z, CORE, Y_LO, X), ("y_hi", "z", "core", "y_lo", "x")
    )
    cell, gene = ("y_hi", "z", "core"), ("y_lo", "x")
    in_specs = (P(cell, gene), P(cell), P(gene), P(gene, cell))
    out_specs = (P(cell, None), P(gene, None))
    return jax.shard_map(shards, mesh=fine, in_specs=in_specs, out_specs=out_specs, check_vma=False)
```

```python
import math

import jax
import jax.numpy as jnp
import numpy as np
from jax import lax
from jax.sharding import Mesh, PartitionSpec as P

ITERS = 3
Y_HI, Z, CORE, Y_LO, X = 2, 8, 2, 4, 4
BLOCKS = CORE * Y_HI
EXTRA = 8
F32, BF16 = jnp.float32, jnp.bfloat16


def spread(x, axis, n):
    return lax.all_to_all(jnp.broadcast_to(x[None], (n,) + x.shape), axis, 0, 0, tiled=True)


def gather_sum(x, axis, n, factor=None):
    total = jnp.sum(spread(x, axis, n).astype(F32), axis=0)
    if factor is not None:
        total = total * factor
    return total.astype(BF16)


def shards(counts, cell_totals, gene_totals, test_matrix):
    rows, cols = counts.shape
    scale = 1.0 / math.sqrt(rows * Y_HI * Z * CORE + cols * Y_LO * X)

    pieces = jnp.stack([cell_totals >> shift & 2047 for shift in (0, 11, 22)])
    extra = jnp.zeros((EXTRA, cols), jnp.int16).at[:3, :rows].set(pieces.astype(jnp.int16))
    mine = jnp.concatenate([counts.astype(jnp.int16), extra])
    other = lax.ppermute(mine, "y_hi", [(0, 1), (1, 0)])

    totals = lax.all_to_all(
        jnp.broadcast_to(gene_totals[None], (Y_LO * X, cols)), ("y_lo", "x"), 0, 0, tiled=True
    )
    total = jnp.sum(totals)
    fraction = gene_totals.astype(F32) / total.astype(F32)
    test = spread(test_matrix.T, "z", Z).reshape(Z * test_matrix.shape[1], cols)

    blocks = lax.all_gather(jnp.stack([mine, other]), "core").reshape(BLOCKS, rows + EXTRA, cols)
    pieces = blocks[:, rows : rows + 3, :rows].astype(jnp.int32)
    owned = (pieces[:, 0] + (pieces[:, 1] << 11) + (pieces[:, 2] << 22)).astype(F32)
    expected = owned[:, :, None] * fraction[None, None, :]
    stored = (
        (blocks[:, :rows].astype(F32) - expected)
        / jnp.sqrt(expected + expected * expected / 100.0)
    ).astype(BF16)
    stored = stored.reshape(BLOCKS * rows, cols)

    def cell_side(panel, factor):
        part = lax.dot_general(
            panel, stored, (((1,), (1,)), ((), ())), preferred_element_type=F32
        ).astype(BF16)
        return gather_sum(gather_sum(part, "x", X), "y_lo", Y_LO, factor)

    def gene_side(sketch):
        part = jnp.dot(sketch, stored, preferred_element_type=F32).astype(BF16)
        return gather_sum(part, "z", Z, scale)

    sketch = cell_side(test, 1.0)
    for step in range(ITERS):
        panel = gene_side(sketch)
        sketch = cell_side(panel, scale)
    gene_panel = gene_side(sketch)

    width = sketch.shape[0]
    parts = sketch.reshape(width, CORE, Y_HI, rows)
    parts = jnp.where(lax.axis_index("y_hi") == 0, parts, parts[:, :, ::-1])
    parts = parts.reshape(width, BLOCKS, rows).transpose(1, 0, 2)
    send = jnp.concatenate(
        [parts, jnp.broadcast_to(gene_panel[None], (BLOCKS, width, cols))], axis=2
    )
    got = lax.all_to_all(send, ("core", "y_hi"), 0, 0, tiled=True)
    got = got.reshape(CORE, Y_HI, Z, width // Z, rows + cols).transpose(1, 2, 0, 3, 4)
    got = got.reshape(BLOCKS * width, rows + cols)
    return (got[:, :rows].T, got[:, rows:].T)


def solution(mesh):
    fine = Mesh(
        np.asarray(mesh.devices).reshape(Y_HI, Z, CORE, Y_LO, X), ("y_hi", "z", "core", "y_lo", "x")
    )
    cell, gene = ("y_hi", "z", "core"), ("y_lo", "x")
    in_specs = (P(cell, gene), P(cell), P(gene), P(gene, cell))
    out_specs = (P(cell, None), P(gene, None))
    return jax.shard_map(shards, mesh=fine, in_specs=in_specs, out_specs=out_specs, check_vma=False)
```

```python
import math

import jax
import jax.numpy as jnp
import numpy as np
from jax import lax
from jax.sharding import Mesh, PartitionSpec as P

ITERS = 3
Y_HI, Z, CORE, Y_LO, X_HI, X_LO = 2, 8, 2, 4, 2, 2
X, BLOCKS, EXTRA = X_HI * X_LO, CORE * Y_HI, 8
F32, BF16, I16 = jnp.float32, jnp.bfloat16, jnp.int16
PAIRS = ((0, 3), (1, 2))


def copies(x, n):
    return jnp.broadcast_to(x[None], (n,) + x.shape)


def spread(x, axis, n):
    return lax.all_to_all(copies(x, n), axis, 0, 0, tiled=True)


def gather_sum(x, axis, n, factor=None):
    got = spread(x, axis, n)
    total = got[0].astype(F32)
    for i in range(1, n):
        total = total + got[i].astype(F32)
    if factor is not None:
        total = total * factor
    return total.astype(BF16)


def shards(counts, cell_totals, gene_totals, test_matrix):
    rows, cols = counts.shape
    scale = 1.0 / math.sqrt(rows * Y_HI * Z * CORE + cols * Y_LO * X)
    x_hi = lax.axis_index("x_hi")

    totals = spread(gene_totals, ("y_lo", "x_hi", "x_lo"), Y_LO * X)
    total = jnp.sum(totals).astype(F32)
    fraction = gene_totals.astype(F32) / total
    place = lax.axis_index(("y_lo", "x_hi", "x_lo"))
    beside = lax.dynamic_index_in_dim(totals, place ^ 3, 0, keepdims=False).astype(F32) / total

    pieces = jnp.stack([cell_totals >> shift & 2047 for shift in (0, 11, 22)])
    extra = jnp.zeros((EXTRA, cols), I16).at[:3, :rows].set(pieces.astype(I16))
    mine = jnp.concatenate([counts.astype(I16), extra])

    def over_y(block):
        return lax.ppermute(block, "y_hi", [(0, 1), (1, 0)])

    def over_x(block):
        return lax.ppermute(block, ("x_hi", "x_lo"), [(i, 3 - i) for i in range(X)])

    def resid(block, fraction):
        both = lax.all_gather(block, "core")
        pieces = both[:, rows : rows + 3, :rows].astype(jnp.int32)
        owned = (pieces[:, 0] + (pieces[:, 1] << 11) + (pieces[:, 2] << 22)).astype(F32)
        expected = owned[:, :, None] * fraction[None, None, :]
        return (
            (both[:, :rows].astype(F32) - expected)
            / jnp.sqrt(expected + expected * expected / 100.0)
        ).astype(BF16)

    other = over_y(mine)
    near = over_x(mine)
    test = spread(test_matrix.T, "z", Z).reshape(Z * test_matrix.shape[1], cols)
    far = over_x(other)

    cells = BLOCKS * rows
    own = jnp.concatenate([resid(mine, fraction), resid(other, fraction)]).reshape(cells, cols)

    def cell_part(panel, stored):
        return lax.dot_general(
            panel, stored, (((1,), (1,)), ((), ())), preferred_element_type=F32
        ).astype(BF16)

    part = gather_sum(cell_part(test, own), ("x_hi", "x_lo"), X)
    width = part.shape[0] // 2
    part = jnp.where(x_hi == 0, part[:width], part[width:])
    sketch = gather_sum(part, "y_lo", Y_LO)

    paired = jnp.concatenate([resid(near, beside), resid(far, beside)]).reshape(cells, cols)
    stored = jnp.concatenate([own, paired], axis=1)

    def gene_side(sketch):
        part = jnp.dot(sketch, stored, preferred_element_type=F32).astype(BF16)
        return gather_sum(part, "z", Z, scale)

    def cell_side(panel):
        return gather_sum(cell_part(panel, stored), ("y_lo", "x_lo"), Y_LO * X_LO, scale)

    for step in range(ITERS):
        sketch = cell_side(gene_side(sketch))
    gene_panel = gene_side(sketch)

    parts = sketch.reshape(width, Y_HI, CORE, rows)
    parts = jnp.where(lax.axis_index("y_hi") == 0, parts, parts[:, ::-1])
    parts = parts.transpose(1, 2, 0, 3)[:, :, None]
    parts = jnp.broadcast_to(parts, (Y_HI, CORE, 2, width, rows))
    halves = gene_panel.reshape(width, 2, cols)
    halves = jnp.where(x_hi == 0, halves, halves[:, ::-1]).transpose(1, 0, 2)
    halves = jnp.broadcast_to(halves, (Y_HI, CORE, 2, width, cols))
    send = jnp.concatenate([parts, halves], axis=4).reshape(BLOCKS * 2, width, rows + cols)
    groups = [
        [(y * CORE + c) * X + x for y in range(Y_HI) for c in range(CORE) for x in pair]
        for pair in PAIRS
    ]
    got = lax.all_to_all(
        send, ("y_hi", "core", "x_hi", "x_lo"), 0, 0, axis_index_groups=groups, tiled=True
    )
    got = got.reshape(Y_HI, CORE, 2, Z // 2, 2 * width // Z, rows + cols).transpose(0, 2, 3, 1, 4, 5)
    got = got.reshape(BLOCKS * 2 * width, rows + cols)
    return (got[:, :rows].T, got[:, rows:].T)


def solution(mesh):
    fine = Mesh(
        np.asarray(mesh.devices).reshape(Y_HI, Z, CORE, Y_LO, X_HI, X_LO),
        ("y_hi", "z", "core", "y_lo", "x_hi", "x_lo"),
    )
    cell, gene = ("y_hi", "z", "core"), ("y_lo", "x_hi", "x_lo")
    in_specs = (P(cell, gene), P(cell), P(gene), P(gene, cell))
    out_specs = (P(cell, None), P(gene, None))
    return jax.shard_map(shards, mesh=fine, in_specs=in_specs, out_specs=out_specs, check_vma=False)
```

```python
import math

import jax
import jax.numpy as jnp
import numpy as np
from jax import lax
from jax.sharding import Mesh, PartitionSpec as P

ITERS = 3
Y_HI, Z, CORE, Y_LO, X = 2, 8, 2, 4, 4
BLOCKS = CORE * Y_HI
EXTRA = 8
F32, BF16, I16 = jnp.float32, jnp.bfloat16, jnp.int16


def copies(x, n):
    return jnp.broadcast_to(x[None], (n,) + x.shape)


def spread(x, axis, n):
    return lax.all_to_all(copies(x, n), axis, 0, 0, tiled=True)


def gather_sum(x, axis, n, factor=None):
    got = spread(x, axis, n)
    total = got[0].astype(F32)
    for i in range(1, n):
        total = total + got[i].astype(F32)
    if factor is not None:
        total = total * factor
    return total.astype(BF16)


def shards(counts, cell_totals, gene_totals, test_matrix):
    rows, cols = counts.shape
    scale = 1.0 / math.sqrt(rows * Y_HI * Z * CORE + cols * Y_LO * X)

    everyone = spread(gene_totals, ("y_lo", "x"), Y_LO * X)

    pieces = jnp.stack([cell_totals >> shift & 2047 for shift in (0, 11, 22)])
    extra = jnp.zeros((EXTRA, cols), I16).at[:3, :rows].set(pieces.astype(I16))
    mine = jnp.concatenate([counts.astype(I16), extra])
    other = lax.ppermute(mine, "y_hi", [(0, 1), (1, 0)])

    total = jnp.sum(everyone).astype(F32)
    fraction = gene_totals.astype(F32) / total
    test, fraction = lax.optimization_barrier((test_matrix.T, fraction))
    test = spread(test, "z", Z).reshape(Z * test_matrix.shape[1], cols)

    def resid(block):
        both = lax.all_gather(block, "core")
        pieces = both[:, rows : rows + 3, :rows].astype(jnp.int32)
        owned = (pieces[:, 0] + (pieces[:, 1] << 11) + (pieces[:, 2] << 22)).astype(F32)
        expected = owned[:, :, None] * fraction[None, None, :]
        return (
            (both[:, :rows].astype(F32) - expected)
            / jnp.sqrt(expected + expected * expected / 100.0)
        ).astype(BF16)

    stored = jnp.concatenate([resid(mine), resid(other)]).reshape(BLOCKS * rows, cols)

    def cell_side(panel, factor):
        part = lax.dot_general(
            panel, stored, (((1,), (1,)), ((), ())), preferred_element_type=F32
        ).astype(BF16)
        return gather_sum(gather_sum(part, "x", X), "y_lo", Y_LO, factor)

    def gene_side(sketch):
        part = jnp.dot(sketch, stored, preferred_element_type=F32).astype(BF16)
        return gather_sum(part, "z", Z, scale)

    sketch = cell_side(test, 1.0)
    for step in range(ITERS):
        panel = gene_side(sketch)
        sketch = cell_side(panel, scale)
    gene_panel = gene_side(sketch)

    width = sketch.shape[0]
    parts = sketch.reshape(width, Y_HI, CORE, rows)
    parts = jnp.where(lax.axis_index("y_hi") == 0, parts, parts[:, ::-1])
    parts = parts.reshape(width, BLOCKS, rows).transpose(1, 0, 2)
    send = jnp.concatenate([parts, copies(gene_panel, BLOCKS)], axis=2)
    got = lax.all_to_all(send, ("y_hi", "core"), 0, 0, tiled=True)
    got = got.reshape(Y_HI, CORE, Z, width // Z, rows + cols).transpose(0, 2, 1, 3, 4)
    got = got.reshape(BLOCKS * width, rows + cols)
    return (got[:, :rows].T, got[:, rows:].T)


def solution(mesh):
    fine = Mesh(
        np.asarray(mesh.devices).reshape(Y_HI, Z, CORE, Y_LO, X), ("y_hi", "z", "core", "y_lo", "x")
    )
    cell, gene = ("y_hi", "z", "core"), ("y_lo", "x")
    in_specs = (P(cell, gene), P(cell), P(gene), P(gene, cell))
    out_specs = (P(cell, None), P(gene, None))
    return jax.shard_map(shards, mesh=fine, in_specs=in_specs, out_specs=out_specs, check_vma=False)
```

```python
import math

import jax
import jax.numpy as jnp
import numpy as np
from jax import lax
from jax.sharding import Mesh, PartitionSpec as P

ITERS = 3
Y_HI, Z, CORE, Y_LO, X = 2, 8, 2, 4, 4
BLOCKS = CORE * Y_HI
EXTRA = 8
F32, BF16, I16 = jnp.float32, jnp.bfloat16, jnp.int16


def copies(x, n):
    return jnp.broadcast_to(x[None], (n,) + x.shape)


def spread(x, axis, n):
    return lax.all_to_all(copies(x, n), axis, 0, 0, tiled=True)


def gather_sum(x, axis, n, factor=None):
    got = spread(x, axis, n)
    total = got[0].astype(F32)
    for i in range(1, n):
        total = total + got[i].astype(F32)
    if factor is not None:
        total = total * factor
    return total.astype(BF16)


def shards(counts, cell_totals, gene_totals, test_matrix):
    rows, cols = counts.shape
    scale = 1.0 / math.sqrt(rows * Y_HI * Z * CORE + cols * Y_LO * X)

    everyone = spread(gene_totals, ("y_lo", "x"), Y_LO * X)

    pieces = jnp.stack([cell_totals >> shift & 2047 for shift in (0, 11, 22)])
    extra = jnp.zeros((EXTRA, cols), I16).at[:3, :rows].set(pieces.astype(I16))
    mine = jnp.concatenate([counts.astype(I16), extra])
    other = lax.ppermute(mine, "y_hi", [(0, 1), (1, 0)])

    total = jnp.sum(everyone).astype(F32)
    fraction = gene_totals.astype(F32) / total
    test, fraction = lax.optimization_barrier((test_matrix.T, fraction))
    ready, held = lax.optimization_barrier((copies(test, Z), mine))
    test = lax.all_to_all(ready, "z", 0, 0, tiled=True).reshape(Z * test_matrix.shape[1], cols)

    def resid(block):
        both = lax.all_gather(block, "core")
        pieces = both[:, rows : rows + 3, :rows].astype(jnp.int32)
        owned = (pieces[:, 0] + (pieces[:, 1] << 11) + (pieces[:, 2] << 22)).astype(F32)
        expected = owned[:, :, None] * fraction[None, None, :]
        return (
            (both[:, :rows].astype(F32) - expected)
            / jnp.sqrt(expected + expected * expected / 100.0)
        ).astype(BF16)

    stored = jnp.concatenate([resid(held), resid(other)]).reshape(BLOCKS * rows, cols)

    def cell_side(panel, factor):
        part = lax.dot_general(
            panel, stored, (((1,), (1,)), ((), ())), preferred_element_type=F32
        ).astype(BF16)
        return gather_sum(gather_sum(part, "x", X), "y_lo", Y_LO, factor)

    def gene_side(sketch):
        part = jnp.dot(sketch, stored, preferred_element_type=F32).astype(BF16)
        return gather_sum(part, "z", Z, scale)

    sketch = cell_side(test, 1.0)
    for step in range(ITERS):
        panel = gene_side(sketch)
        sketch = cell_side(panel, scale)
    gene_panel = gene_side(sketch)

    width = sketch.shape[0]
    parts = sketch.reshape(width, Y_HI, CORE, rows)
    parts = jnp.where(lax.axis_index("y_hi") == 0, parts, parts[:, ::-1])
    parts = parts.reshape(width, BLOCKS, rows).transpose(1, 0, 2)
    send = jnp.concatenate([parts, copies(gene_panel, BLOCKS)], axis=2)
    got = lax.all_to_all(send, ("y_hi", "core"), 0, 0, tiled=True)
    got = got.reshape(Y_HI, CORE, Z, width // Z, rows + cols).transpose(0, 2, 1, 3, 4)
    got = got.reshape(BLOCKS * width, rows + cols)
    return (got[:, :rows].T, got[:, rows:].T)


def solution(mesh):
    fine = Mesh(
        np.asarray(mesh.devices).reshape(Y_HI, Z, CORE, Y_LO, X), ("y_hi", "z", "core", "y_lo", "x")
    )
    cell, gene = ("y_hi", "z", "core"), ("y_lo", "x")
    in_specs = (P(cell, gene), P(cell), P(gene), P(gene, cell))
    out_specs = (P(cell, None), P(gene, None))
    return jax.shard_map(shards, mesh=fine, in_specs=in_specs, out_specs=out_specs, check_vma=False)
```

```python
import math

import jax
import jax.numpy as jnp
import numpy as np
from jax import lax
from jax.sharding import Mesh, PartitionSpec as P

ITERS = 3
Y_HI, Z, CORE, Y_LO, X_HI, X_LO = 2, 8, 2, 4, 2, 2
X, BLOCKS, EXTRA = X_HI * X_LO, CORE * Y_HI, 8
F32, BF16, I16 = jnp.float32, jnp.bfloat16, jnp.int16
PAIRS = ((0, 3), (1, 2))


def copies(x, n):
    return jnp.broadcast_to(x[None], (n,) + x.shape)


def spread(x, axis, n):
    return lax.all_to_all(copies(x, n), axis, 0, 0, tiled=True)


def total_of(got, factor=None):
    total = got[0].astype(F32)
    for i in range(1, got.shape[0]):
        total = total + got[i].astype(F32)
    if factor is not None:
        total = total * factor
    return total.astype(BF16)


def gather_sum(x, axis, n, factor=None):
    shape = x.shape
    got = spread(x.reshape(-1, 4, shape[1]) if shape[0] % 8 else x, axis, n)
    return total_of(got, factor).reshape(shape)


def shards(counts, cell_totals, gene_totals, test_matrix):
    rows, cols = counts.shape
    scale = 1.0 / math.sqrt(rows * Y_HI * Z * CORE + cols * Y_LO * X)
    x_hi = lax.axis_index("x_hi")

    pieces = jnp.stack([cell_totals >> shift & 2047 for shift in (0, 11, 22)])
    extra = jnp.zeros((EXTRA, cols), I16).at[:3, :rows].set(pieces.astype(I16))
    mine = jnp.concatenate([counts.astype(I16), extra])

    def both(block):
        return lax.all_gather(block, "core")

    def over_y(block):
        return lax.ppermute(block, "y_hi", [(0, 1), (1, 0)])

    def over_x(block):
        return lax.ppermute(block, ("x_hi", "x_lo"), [(i, 3 - i) for i in range(X)])

    def resid(both, fraction):
        pieces = both[:, rows : rows + 3, :rows].astype(jnp.int32)
        owned = (pieces[:, 0] + (pieces[:, 1] << 11) + (pieces[:, 2] << 22)).astype(F32)
        expected = owned[:, :, None] * fraction[None, None, :]
        return (
            (both[:, :rows].astype(F32) - expected)
            / jnp.sqrt(expected + expected * expected / 100.0)
        ).astype(BF16)

    cut = rows // 2
    other = [over_y(mine[:cut]), over_y(mine[cut:])]
    near = over_x(mine)
    ready, first = lax.optimization_barrier((copies(gene_totals, Y_LO * X), other[0]))
    totals = lax.all_to_all(ready, ("y_lo", "x_hi", "x_lo"), 0, 0, tiled=True)
    total = jnp.sum(totals).astype(F32)
    fraction = gene_totals.astype(F32) / total
    place = lax.axis_index(("y_lo", "x_hi", "x_lo"))
    beside = lax.dynamic_index_in_dim(totals, place ^ 3, 0, keepdims=False).astype(F32) / total
    ready, held = lax.optimization_barrier((copies(test_matrix.T, Z), mine))
    test = lax.all_to_all(ready, "z", 0, 0, tiled=True).reshape(Z * test_matrix.shape[1], cols)
    near = both(near)
    near, last = lax.optimization_barrier((near, other[1]))
    other = [first, last]
    far = [over_x(chunk) for chunk in other]

    cells = BLOCKS * rows
    own = [resid(both(held), fraction), resid(both(jnp.concatenate(other)), fraction)]
    own = jnp.concatenate(own).reshape(cells, cols)

    def cell_part(panel, stored):
        return lax.dot_general(
            panel, stored, (((1,), (1,)), ((), ())), preferred_element_type=F32
        )

    ready, far = lax.optimization_barrier((copies(cell_part(test, own).astype(BF16), X), far))
    part = total_of(lax.all_to_all(ready, ("x_hi", "x_lo"), 0, 0, tiled=True))
    width = part.shape[0] // 2
    part = jnp.where(x_hi == 0, part[:width], part[width:])
    sketch = gather_sum(part, "y_lo", Y_LO)

    paired = [resid(near, beside), resid(both(jnp.concatenate(far)), beside)]
    paired = jnp.concatenate(paired).reshape(cells, cols)

    def gene_side(sketch):
        part = jnp.concatenate(
            [jnp.dot(sketch, stored, preferred_element_type=F32) for stored in (own, paired)], axis=1
        )
        return gather_sum(part.astype(BF16), "z", Z, scale)

    def cell_side(panel):
        part = cell_part(panel[:, :cols], own) + cell_part(panel[:, cols:], paired)
        return gather_sum(part.astype(BF16), ("y_lo", "x_lo"), Y_LO * X_LO, scale)

    for step in range(ITERS):
        sketch = cell_side(gene_side(sketch))
    gene_panel = gene_side(sketch)

    parts = sketch.reshape(width, Y_HI, CORE, rows)
    parts = jnp.where(lax.axis_index("y_hi") == 0, parts, parts[:, ::-1])
    parts = parts.transpose(1, 2, 0, 3)[:, :, None]
    parts = jnp.broadcast_to(parts, (Y_HI, CORE, 2, width, rows))
    halves = gene_panel.reshape(width, 2, cols)
    halves = jnp.where(x_hi == 0, halves, halves[:, ::-1]).transpose(1, 0, 2)
    halves = jnp.broadcast_to(halves, (Y_HI, CORE, 2, width, cols))
    send = jnp.concatenate([parts, halves], axis=4).reshape(BLOCKS * 2, width, rows + cols)
    groups = [
        [(y * CORE + c) * X + x for y in range(Y_HI) for c in range(CORE) for x in pair]
        for pair in PAIRS
    ]
    got = lax.all_to_all(
        send, ("y_hi", "core", "x_hi", "x_lo"), 0, 0, axis_index_groups=groups, tiled=True
    )
    got = got.reshape(Y_HI, CORE, 2, Z // 2, 2 * width // Z, rows + cols).transpose(0, 2, 3, 1, 4, 5)
    got = got.reshape(BLOCKS * 2 * width, rows + cols)
    return (got[:, :rows].T, got[:, rows:].T)


def solution(mesh):
    fine = Mesh(
        np.asarray(mesh.devices).reshape(Y_HI, Z, CORE, Y_LO, X_HI, X_LO),
        ("y_hi", "z", "core", "y_lo", "x_hi", "x_lo"),
    )
    cell, gene = ("y_hi", "z", "core"), ("y_lo", "x_hi", "x_lo")
    in_specs = (P(cell, gene), P(cell), P(gene), P(gene, cell))
    out_specs = (P(cell, None), P(gene, None))
    return jax.shard_map(shards, mesh=fine, in_specs=in_specs, out_specs=out_specs, check_vma=False)
```

```python
import math

import jax
import jax.numpy as jnp
import numpy as np
from jax import lax
from jax.sharding import Mesh, PartitionSpec as P

ITERS = 3
Y_HI, Z, CORE, Y_LO, X = 2, 8, 2, 4, 4
BLOCKS = CORE * Y_HI
EXTRA = 8
F32, BF16, I16 = jnp.float32, jnp.bfloat16, jnp.int16


def copies(x, n):
    return jnp.broadcast_to(x[None], (n,) + x.shape)


def spread(x, axis, n):
    return lax.all_to_all(copies(x, n), axis, 0, 0, tiled=True)


def gather_sum(x, axis, n, factor=None):
    got = spread(x, axis, n)
    total = got[0].astype(F32)
    for i in range(1, n):
        total = total + got[i].astype(F32)
    if factor is not None:
        total = total * factor
    return total.astype(BF16)


def shards(counts, cell_totals, gene_totals, test_matrix):
    rows, cols = counts.shape
    scale = 1.0 / math.sqrt(rows * Y_HI * Z * CORE + cols * Y_LO * X)

    def over_y(block):
        return lax.ppermute(block, "y_hi", [(0, 1), (1, 0)])

    mine = counts.astype(I16)
    other = over_y(mine)
    held, cell_totals = lax.optimization_barrier((mine, cell_totals))
    pieces = jnp.stack([cell_totals >> shift & 2047 for shift in (0, 11, 22)])
    pieces = jnp.zeros((EXTRA, cols), I16).at[:3, :rows].set(pieces.astype(I16))
    beyond = over_y(pieces)

    ready, held, pieces = lax.optimization_barrier((copies(test_matrix.T, Z), held, pieces))
    test = lax.all_to_all(ready, "z", 0, 0, tiled=True).reshape(Z * test_matrix.shape[1], cols)
    ready, test = lax.optimization_barrier((copies(gene_totals, Y_LO * X), test))
    everyone = lax.all_to_all(ready, ("y_lo", "x"), 0, 0, tiled=True)
    total = jnp.sum(everyone).astype(F32)
    fraction = gene_totals.astype(F32) / total

    def resid(block, pieces):
        both = lax.all_gather(jnp.concatenate([block, pieces]), "core")
        pieces = both[:, rows : rows + 3, :rows].astype(jnp.int32)
        owned = (pieces[:, 0] + (pieces[:, 1] << 11) + (pieces[:, 2] << 22)).astype(F32)
        expected = owned[:, :, None] * fraction[None, None, :]
        return (
            (both[:, :rows].astype(F32) - expected)
            / jnp.sqrt(expected + expected * expected / 100.0)
        ).astype(BF16)

    stored = jnp.concatenate([resid(held, pieces), resid(other, beyond)])
    stored = stored.reshape(BLOCKS * rows, cols)

    def cell_side(panel, factor):
        part = lax.dot_general(
            panel, stored, (((1,), (1,)), ((), ())), preferred_element_type=F32
        ).astype(BF16)
        return gather_sum(gather_sum(part, "x", X), "y_lo", Y_LO, factor)

    def gene_side(sketch):
        part = jnp.dot(sketch, stored, preferred_element_type=F32).astype(BF16)
        return gather_sum(part, "z", Z, scale)

    sketch = cell_side(test, 1.0)
    for step in range(ITERS):
        panel = gene_side(sketch)
        sketch = cell_side(panel, scale)
    gene_panel = gene_side(sketch)

    sketch, gene_panel = lax.optimization_barrier((sketch, gene_panel))
    half = CORE * rows
    near, far = sketch[:, :half], sketch[:, half:]
    low = lax.axis_index("y_hi") == 0
    parts = jnp.concatenate([jnp.where(low, near, far), jnp.where(low, far, near)], axis=1)
    send = jnp.stack(
        [
            jnp.concatenate([parts[:, i * rows : (i + 1) * rows], gene_panel], axis=1)
            for i in range(BLOCKS)
        ]
    )
    got = lax.all_to_all(send, ("y_hi", "core"), 0, 0, tiled=True)
    got = got.reshape(-1, rows + cols)
    count = got.shape[0]
    order = np.arange(count).reshape(Y_HI, CORE, Z, -1).transpose(0, 2, 1, 3).reshape(-1)
    pick = jnp.asarray(np.eye(count)[order], BF16)

    def ordered(block):
        return jnp.dot(pick, block, preferred_element_type=F32).astype(BF16).T

    return (ordered(got[:, :rows]), ordered(got[:, rows:]))


def solution(mesh):
    fine = Mesh(
        np.asarray(mesh.devices).reshape(Y_HI, Z, CORE, Y_LO, X), ("y_hi", "z", "core", "y_lo", "x")
    )
    cell, gene = ("y_hi", "z", "core"), ("y_lo", "x")
    in_specs = (P(cell, gene), P(cell), P(gene), P(gene, cell))
    out_specs = (P(cell, None), P(gene, None))
    return jax.shard_map(shards, mesh=fine, in_specs=in_specs, out_specs=out_specs, check_vma=False)
```

```python
import math

import jax
import jax.numpy as jnp
import numpy as np
from jax import lax
from jax.sharding import Mesh, PartitionSpec as P

ITERS = 3
Y_HI, Z, CORE, Y_LO, X = 2, 8, 2, 4, 4
BLOCKS = CORE * Y_HI
EXTRA = 8
F32, BF16, I16 = jnp.float32, jnp.bfloat16, jnp.int16


def copies(x, n):
    return jnp.broadcast_to(x[None], (n,) + x.shape)


def spread(x, axis, n):
    return lax.all_to_all(copies(x, n), axis, 0, 0)


def gather_sum(x, axis, n, factor=None):
    got = spread(x, axis, n)
    total = got[0].astype(F32)
    for i in range(1, n):
        total = total + got[i].astype(F32)
    if factor is not None:
        total = total * factor
    return total.astype(BF16)


def shards(counts, cell_totals, gene_totals, test_matrix):
    rows, cols = counts.shape
    scale = 1.0 / math.sqrt(rows * Y_HI * Z * CORE + cols * Y_LO * X)

    pieces = jnp.stack([cell_totals >> shift & 2047 for shift in (0, 11, 22)])
    extra = jnp.zeros((EXTRA, cols), I16).at[:3, :rows].set(pieces.astype(I16))
    mine = jnp.concatenate([counts.astype(I16), extra])
    other = lax.ppermute(mine, "y_hi", [(0, 1), (1, 0)])

    test = spread(test_matrix.T, "z", Z)
    ready, test = lax.optimization_barrier((gene_totals.reshape(8, -1), test))
    totals = spread(ready, ("y_lo", "x"), Y_LO * X)
    test, totals = lax.optimization_barrier((test, totals))
    test = test.reshape(Z * test_matrix.shape[1], cols)
    total = jnp.sum(totals)
    fraction = gene_totals.astype(F32) / total.astype(F32)

    low = lax.axis_index("y_hi") == 0
    pair = jnp.stack([jnp.where(low, mine, other), jnp.where(low, other, mine)])
    blocks = lax.all_gather(pair, "core").reshape(BLOCKS, rows + EXTRA, cols)
    pieces = blocks[:, rows : rows + 3, :rows].astype(jnp.int32)
    owned = (pieces[:, 0] + (pieces[:, 1] << 11) + (pieces[:, 2] << 22)).astype(F32)
    expected = owned[:, :, None] * fraction[None, None, :]
    stored = (
        (blocks[:, :rows].astype(F32) - expected)
        / jnp.sqrt(expected + expected * expected / 100.0)
    ).astype(BF16)
    stored = stored.reshape(BLOCKS * rows, cols)

    def cell_side(panel, factor):
        part = lax.dot_general(
            panel, stored, (((1,), (1,)), ((), ())), preferred_element_type=F32
        ).astype(BF16)
        return gather_sum(gather_sum(part, "x", X), "y_lo", Y_LO, factor)

    def gene_side(sketch):
        part = jnp.dot(sketch, stored, preferred_element_type=F32).astype(BF16)
        return gather_sum(part, "z", Z, scale)

    sketch = cell_side(test, 1.0)
    for step in range(ITERS):
        panel = gene_side(sketch)
        sketch = cell_side(panel, scale)
    gene_panel = gene_side(sketch)

    width = sketch.shape[0]
    count = BLOCKS * width
    order = np.arange(count).reshape(CORE, Y_HI, Z, -1).transpose(1, 2, 0, 3).reshape(-1)
    pick = jnp.asarray(np.eye(count)[order], BF16)
    sketch, gene_panel = lax.optimization_barrier((sketch, gene_panel))
    send = jnp.stack(
        [
            jnp.concatenate([sketch[:, i * rows : (i + 1) * rows], gene_panel], axis=1)
            for i in range(BLOCKS)
        ]
    )
    got = lax.all_to_all(send, ("core", "y_hi"), 0, 0)
    got = got.reshape(-1, rows + cols)

    def ordered(block):
        return jnp.dot(pick, block, preferred_element_type=F32).astype(BF16).T

    return (ordered(got[:, :rows]), ordered(got[:, rows:]))


def solution(mesh):
    fine = Mesh(
        np.asarray(mesh.devices).reshape(Y_HI, Z, CORE, Y_LO, X), ("y_hi", "z", "core", "y_lo", "x")
    )
    cell, gene = ("y_hi", "z", "core"), ("y_lo", "x")
    in_specs = (P(cell, gene), P(cell), P(gene), P(gene, cell))
    out_specs = (P(cell, None), P(gene, None))
    return jax.shard_map(shards, mesh=fine, in_specs=in_specs, out_specs=out_specs, check_vma=False)
```

```python
import math

import jax
import jax.numpy as jnp
import numpy as np
from jax import lax
from jax.sharding import Mesh, PartitionSpec as P

ITERS = 3
Y_HI, Z, CORE, Y_LO, X = 2, 8, 2, 4, 4
BLOCKS = CORE * Y_HI
EXTRA = 8
F32, BF16, I16 = jnp.float32, jnp.bfloat16, jnp.int16


def copies(x, n):
    return jnp.broadcast_to(x[None], (n,) + x.shape)


def spread(x, axis, n):
    return lax.all_to_all(copies(x, n), axis, 0, 0)


def gather_sum(x, axis, n, factor=None):
    got = spread(x, axis, n)
    total = got[0].astype(F32)
    for i in range(1, n):
        total = total + got[i].astype(F32)
    if factor is not None:
        total = total * factor
    return total.astype(BF16)


def shards(counts, cell_totals, gene_totals, test_matrix):
    rows, cols = counts.shape
    scale = 1.0 / math.sqrt(rows * Y_HI * Z * CORE + cols * Y_LO * X)

    def over_y(block):
        return lax.ppermute(block, "y_hi", [(0, 1), (1, 0)])

    def over_core(block):
        return lax.all_gather(block, "core")

    mine = counts.astype(I16)
    other = over_y(mine)
    ready, held = lax.optimization_barrier((gene_totals.reshape(8, -1), mine))
    totals = spread(ready, ("y_lo", "x"), Y_LO * X)

    test, held = lax.optimization_barrier((test_matrix.T, held))
    for axis in ("z_lo", "z_mid", "z_hi"):
        test = lax.all_gather(test, axis)
        if axis == "z_lo":
            test, cell_totals = lax.optimization_barrier((test, cell_totals))
            pieces = jnp.stack([cell_totals >> shift & 2047 for shift in (0, 11, 22)])
            pieces = jnp.zeros((EXTRA, cols), I16).at[:3, :rows].set(pieces.astype(I16))
            beyond = over_y(pieces)
    test = test.reshape(Z * test_matrix.shape[1], cols)
    own = over_core(jnp.concatenate([held, pieces]))

    test, totals = lax.optimization_barrier((test, totals))
    fraction = gene_totals.astype(F32) / jnp.sum(totals).astype(F32)
    other = over_core(jnp.concatenate([other, beyond]))

    low = lax.axis_index("y_hi") == 0
    blocks = jnp.stack([jnp.where(low, own, other), jnp.where(low, other, own)], axis=1)
    blocks = blocks.reshape(BLOCKS, rows + EXTRA, cols)
    pieces = blocks[:, rows : rows + 3, :rows].astype(jnp.int32)
    owned = (pieces[:, 0] + (pieces[:, 1] << 11) + (pieces[:, 2] << 22)).astype(F32)
    expected = owned[:, :, None] * fraction[None, None, :]
    stored = (
        (blocks[:, :rows].astype(F32) - expected)
        / jnp.sqrt(expected + expected * expected / 100.0)
    ).astype(BF16)
    stored = stored.reshape(BLOCKS * rows, cols)

    def cell_side(panel, factor):
        part = lax.dot_general(
            panel, stored, (((1,), (1,)), ((), ())), preferred_element_type=F32
        ).astype(BF16)
        return gather_sum(gather_sum(part, "x", X), "y_lo", Y_LO, factor)

    def gene_side(sketch):
        part = jnp.dot(sketch, stored, preferred_element_type=F32).astype(BF16)
        return gather_sum(part, ("z_hi", "z_mid", "z_lo"), Z, scale)

    sketch = cell_side(test, 1.0)
    for step in range(ITERS):
        panel = gene_side(sketch)
        sketch = cell_side(panel, scale)
    gene_panel = gene_side(sketch)

    width = sketch.shape[0]
    count = BLOCKS * width
    order = np.arange(count).reshape(CORE, Y_HI, Z, -1).transpose(1, 2, 0, 3).reshape(-1)
    pick = jnp.asarray(np.eye(count)[order], BF16)
    sketch, gene_panel = lax.optimization_barrier((sketch, gene_panel))
    send = jnp.stack(
        [
            jnp.concatenate([sketch[:, i * rows : (i + 1) * rows], gene_panel], axis=1)
            for i in range(BLOCKS)
        ]
    )
    got = lax.all_to_all(send, ("core", "y_hi"), 0, 0)
    got = got.reshape(-1, rows + cols)

    def ordered(block):
        return jnp.dot(pick, block, preferred_element_type=F32).astype(BF16).T

    return (ordered(got[:, :rows]), ordered(got[:, rows:]))


def solution(mesh):
    fine = Mesh(
        np.asarray(mesh.devices).reshape(Y_HI, 2, 2, 2, CORE, Y_LO, X),
        ("y_hi", "z_hi", "z_mid", "z_lo", "core", "y_lo", "x"),
    )
    cell, gene = ("y_hi", "z_hi", "z_mid", "z_lo", "core"), ("y_lo", "x")
    in_specs = (P(cell, gene), P(cell), P(gene), P(gene, cell))
    out_specs = (P(cell, None), P(gene, None))
    return jax.shard_map(shards, mesh=fine, in_specs=in_specs, out_specs=out_specs, check_vma=False)
```

```python
import math

import jax
import jax.numpy as jnp
import numpy as np
from jax import lax
from jax.sharding import Mesh, PartitionSpec as P

ITERS = 3
Y_HI, Z, CORE, Y_LO, X = 2, 8, 2, 4, 4
BLOCKS = CORE * Y_HI
EXTRA = 8
F32, BF16, I16 = jnp.float32, jnp.bfloat16, jnp.int16


def copies(x, n):
    return jnp.broadcast_to(x[None], (n,) + x.shape)


def spread(x, axis, n):
    return lax.all_to_all(copies(x, n), axis, 0, 0)


def gather_sum(x, axis, n, factor=None):
    got = spread(x, axis, n)
    total = got[0].astype(F32)
    for i in range(1, n):
        total = total + got[i].astype(F32)
    if factor is not None:
        total = total * factor
    return total.astype(BF16)


def shards(counts, cell_totals, gene_totals, test_matrix):
    rows, cols = counts.shape
    scale = 1.0 / math.sqrt(rows * Y_HI * Z * CORE + cols * Y_LO * X)

    low = lax.axis_index("y_hi") == 0
    pieces = jnp.stack([cell_totals >> shift & 2047 for shift in (0, 11, 22)])
    extra = jnp.zeros((EXTRA, cols), I16).at[:3, :rows].set(pieces.astype(I16))
    extra = extra.at[3].set(low.astype(I16))
    mine = jnp.concatenate([counts.astype(I16), extra])
    other = lax.ppermute(mine, "y_hi", [(0, 1), (1, 0)])

    test = spread(test_matrix.T, "z", Z)
    ready, test = lax.optimization_barrier((gene_totals.reshape(8, -1), test))
    totals = spread(ready, ("y_lo", "x"), Y_LO * X)

    pair = jnp.stack([jnp.where(low, mine, other), jnp.where(low, other, mine)])
    blocks = lax.all_gather(pair, "core").reshape(BLOCKS, rows + EXTRA, cols)
    test, totals, blocks = lax.optimization_barrier((test, totals, blocks))
    test = test.reshape(Z * test_matrix.shape[1], cols)
    total = jnp.sum(totals)
    fraction = gene_totals.astype(F32) / total.astype(F32)

    pieces = blocks[:, rows : rows + 3, :rows].astype(jnp.int32)
    owned = (pieces[:, 0] + (pieces[:, 1] << 11) + (pieces[:, 2] << 22)).astype(F32)
    expected = owned[:, :, None] * fraction[None, None, :]
    stored = (
        (blocks[:, :rows].astype(F32) - expected)
        / jnp.sqrt(expected + expected * expected / 100.0)
    ).astype(BF16)
    stored = stored.reshape(BLOCKS * rows, cols)

    def cell_side(panel, factor):
        part = lax.dot_general(
            panel, stored, (((1,), (1,)), ((), ())), preferred_element_type=F32
        ).astype(BF16)
        return gather_sum(gather_sum(part, "x", X), "y_lo", Y_LO, factor)

    def gene_side(sketch):
        part = jnp.dot(sketch, stored, preferred_element_type=F32).astype(BF16)
        return gather_sum(part, "z", Z, scale)

    sketch = cell_side(test, 1.0)
    for step in range(ITERS):
        panel = gene_side(sketch)
        sketch = cell_side(panel, scale)
    gene_panel = gene_side(sketch)

    width = sketch.shape[0]
    count = BLOCKS * width
    order = np.arange(count).reshape(CORE, Y_HI, Z, -1).transpose(1, 2, 0, 3).reshape(-1)
    pick = jnp.asarray(np.eye(count)[order], BF16)
    sketch, gene_panel = lax.optimization_barrier((sketch, gene_panel))
    send = jnp.stack(
        [
            jnp.concatenate([sketch[:, i * rows : (i + 1) * rows], gene_panel], axis=1)
            for i in range(BLOCKS)
        ]
    )
    got = lax.all_to_all(send, ("core", "y_hi"), 0, 0)
    got = got.reshape(-1, rows + cols)

    def ordered(block):
        return jnp.dot(pick, block, preferred_element_type=F32).astype(BF16).T

    return (ordered(got[:, :rows]), ordered(got[:, rows:]))


def solution(mesh):
    fine = Mesh(
        np.asarray(mesh.devices).reshape(Y_HI, Z, CORE, Y_LO, X), ("y_hi", "z", "core", "y_lo", "x")
    )
    cell, gene = ("y_hi", "z", "core"), ("y_lo", "x")
    in_specs = (P(cell, gene), P(cell), P(gene), P(gene, cell))
    out_specs = (P(cell, None), P(gene, None))
    return jax.shard_map(shards, mesh=fine, in_specs=in_specs, out_specs=out_specs, check_vma=False)
```

```python
import math

import jax
import jax.numpy as jnp
import numpy as np
from jax import lax
from jax.sharding import Mesh, PartitionSpec as P

ITERS = 3
Y_HI, Z, CORE, Y_LO, X = 2, 8, 2, 4, 4
BLOCKS = CORE * Y_HI
EXTRA = 8
F32, BF16, I16 = jnp.float32, jnp.bfloat16, jnp.int16


def copies(x, n):
    return jnp.broadcast_to(x[None], (n,) + x.shape)


def spread(x, axis, n):
    return lax.all_to_all(copies(x, n), axis, 0, 0)


def gather_sum(x, axis, n, factor=None):
    got = spread(x, axis, n)
    total = got[0].astype(F32)
    for i in range(1, n):
        total = total + got[i].astype(F32)
    if factor is not None:
        total = total * factor
    return total.astype(BF16)


def shards(counts, cell_totals, gene_totals, test_matrix):
    rows, cols = counts.shape
    scale = 1.0 / math.sqrt(rows * Y_HI * Z * CORE + cols * Y_LO * X)

    pieces = jnp.stack([cell_totals >> shift & 2047 for shift in (0, 11, 22)])
    extra = jnp.zeros((EXTRA, cols), I16).at[:3, :rows].set(pieces.astype(I16))
    mine = jnp.concatenate([counts.astype(I16), extra])
    other = lax.ppermute(mine, "y_hi", [(0, 1), (1, 0)])

    test = spread(test_matrix.T, "z", Z)
    ready, test = lax.optimization_barrier((gene_totals.reshape(8, -1), test))
    totals = spread(jnp.sum(ready, axis=0, keepdims=True), ("y_lo", "x"), Y_LO * X)
    test, totals = lax.optimization_barrier((test, totals))
    test = test.reshape(Z * test_matrix.shape[1], cols)
    total = jnp.sum(totals)
    fraction = gene_totals.astype(F32) / total.astype(F32)

    low = lax.axis_index("y_hi") == 0
    pair = jnp.stack([jnp.where(low, mine, other), jnp.where(low, other, mine)])
    blocks = lax.all_gather(pair, "core").reshape(BLOCKS, rows + EXTRA, cols)
    pieces = blocks[:, rows : rows + 3, :rows].astype(jnp.int32)
    owned = (pieces[:, 0] + (pieces[:, 1] << 11) + (pieces[:, 2] << 22)).astype(F32)
    expected = owned[:, :, None] * fraction[None, None, :]
    stored = (
        (blocks[:, :rows].astype(F32) - expected)
        / jnp.sqrt(expected + expected * expected / 100.0)
    ).astype(BF16)
    stored = stored.reshape(BLOCKS * rows, cols)

    def cell_side(panel, factor):
        part = lax.dot_general(
            panel, stored, (((1,), (1,)), ((), ())), preferred_element_type=F32
        ).astype(BF16)
        return gather_sum(gather_sum(part, "x", X), "y_lo", Y_LO, factor)

    def gene_side(sketch):
        part = jnp.dot(sketch, stored, preferred_element_type=F32).astype(BF16)
        return gather_sum(part, "z", Z, scale)

    sketch = cell_side(test, 1.0)
    for step in range(ITERS):
        panel = gene_side(sketch)
        sketch = cell_side(panel, scale)
    gene_panel = gene_side(sketch)

    width = sketch.shape[0]
    count = BLOCKS * width
    order = np.arange(count).reshape(CORE, Y_HI, Z, -1).transpose(1, 2, 0, 3).reshape(-1)
    pick = jnp.asarray(np.eye(count)[order], BF16)
    sketch, gene_panel = lax.optimization_barrier((sketch, gene_panel))
    send = jnp.stack(
        [
            jnp.concatenate([sketch[:, i * rows : (i + 1) * rows], gene_panel], axis=1)
            for i in range(BLOCKS)
        ]
    )
    got = lax.all_to_all(send, ("core", "y_hi"), 0, 0)
    got = got.reshape(-1, rows + cols)

    def ordered(block):
        return jnp.dot(pick, block, preferred_element_type=F32).astype(BF16).T

    return (ordered(got[:, :rows]), ordered(got[:, rows:]))


def solution(mesh):
    fine = Mesh(
        np.asarray(mesh.devices).reshape(Y_HI, Z, CORE, Y_LO, X), ("y_hi", "z", "core", "y_lo", "x")
    )
    cell, gene = ("y_hi", "z", "core"), ("y_lo", "x")
    in_specs = (P(cell, gene), P(cell), P(gene), P(gene, cell))
    out_specs = (P(cell, None), P(gene, None))
    return jax.shard_map(shards, mesh=fine, in_specs=in_specs, out_specs=out_specs, check_vma=False)
```

```python
import math

import jax
import jax.numpy as jnp
import numpy as np
from jax import lax
from jax.sharding import Mesh, PartitionSpec as P

ITERS = 3
Y_HI, Z, CORE, Y_LO, X = 2, 8, 2, 4, 4
BLOCKS = CORE * Y_HI
EXTRA = 8
F32, BF16, I16 = jnp.float32, jnp.bfloat16, jnp.int16


def copies(x, n):
    return jnp.broadcast_to(x[None], (n,) + x.shape)


def spread(x, axis, n):
    return lax.all_to_all(copies(x, n), axis, 0, 0)


def gather_sum(x, axis, n, factor=None):
    got = spread(x, axis, n)
    total = got[0].astype(F32)
    for i in range(1, n):
        total = total + got[i].astype(F32)
    if factor is not None:
        total = total * factor
    return total.astype(BF16)


def shards(counts, cell_totals, gene_totals, test_matrix):
    rows, cols = counts.shape
    scale = 1.0 / math.sqrt(rows * Y_HI * Z * CORE + cols * Y_LO * X)

    low = lax.axis_index("y_hi") == 0
    pieces = jnp.stack([cell_totals >> shift & 2047 for shift in (0, 11, 22)])
    extra = jnp.zeros((EXTRA, cols), I16).at[:3, :rows].set(pieces.astype(I16))
    extra = extra.at[3].set(low.astype(I16))
    mine = jnp.concatenate([counts.astype(I16), extra])
    other = lax.ppermute(mine, "y_hi", [(0, 1), (1, 0)])

    test = spread(test_matrix.T, "z", Z)
    ready, test = lax.optimization_barrier((gene_totals.reshape(8, -1), test))
    totals = spread(jnp.sum(ready, axis=0, keepdims=True), ("y_lo", "x"), Y_LO * X)
    test, totals = lax.optimization_barrier((test, totals))
    test = test.reshape(Z * test_matrix.shape[1], cols)
    total = jnp.sum(totals)
    fraction = gene_totals.astype(F32) / total.astype(F32)

    pair = jnp.stack([jnp.where(low, mine, other), jnp.where(low, other, mine)])
    blocks = lax.all_gather(pair, "core").reshape(BLOCKS, rows + EXTRA, cols)
    pieces = blocks[:, rows : rows + 3, :rows].astype(jnp.int32)
    owned = (pieces[:, 0] + (pieces[:, 1] << 11) + (pieces[:, 2] << 22)).astype(F32)
    expected = owned[:, :, None] * fraction[None, None, :]
    stored = (
        (blocks[:, :rows].astype(F32) - expected)
        / jnp.sqrt(expected + expected * expected / 100.0)
    ).astype(BF16)
    stored = stored.reshape(BLOCKS * rows, cols)

    def cell_side(panel, factor):
        part = lax.dot_general(
            panel, stored, (((1,), (1,)), ((), ())), preferred_element_type=F32
        ).astype(BF16)
        return gather_sum(gather_sum(part, "x", X), "y_lo", Y_LO, factor)

    def gene_side(sketch):
        part = jnp.dot(sketch, stored, preferred_element_type=F32).astype(BF16)
        return gather_sum(part, "z", Z, scale)

    sketch = cell_side(test, 1.0)
    for step in range(ITERS):
        panel = gene_side(sketch)
        sketch = cell_side(panel, scale)
    gene_panel = gene_side(sketch)

    width = sketch.shape[0]
    count = BLOCKS * width
    order = np.arange(count).reshape(CORE, Y_HI, Z, -1).transpose(1, 2, 0, 3).reshape(-1)
    pick = jnp.asarray(np.eye(count)[order], BF16)
    sketch, gene_panel = lax.optimization_barrier((sketch, gene_panel))
    send = jnp.stack(
        [
            jnp.concatenate([sketch[:, i * rows : (i + 1) * rows], gene_panel], axis=1)
            for i in range(BLOCKS)
        ]
    )
    got = lax.all_to_all(send, ("core", "y_hi"), 0, 0)
    got = got.reshape(-1, rows + cols)

    def ordered(block):
        return jnp.dot(pick, block, preferred_element_type=F32).astype(BF16).T

    return (ordered(got[:, :rows]), ordered(got[:, rows:]))


def solution(mesh):
    fine = Mesh(
        np.asarray(mesh.devices).reshape(Y_HI, Z, CORE, Y_LO, X), ("y_hi", "z", "core", "y_lo", "x")
    )
    cell, gene = ("y_hi", "z", "core"), ("y_lo", "x")
    in_specs = (P(cell, gene), P(cell), P(gene), P(gene, cell))
    out_specs = (P(cell, None), P(gene, None))
    return jax.shard_map(shards, mesh=fine, in_specs=in_specs, out_specs=out_specs, check_vma=False)
```

```python
import math

import jax
import jax.numpy as jnp
import numpy as np
from jax import lax
from jax.sharding import Mesh, PartitionSpec as P

ITERS = 3
Y_HI, Z, CORE, Y_LO, X = 2, 8, 2, 4, 4
BLOCKS = CORE * Y_HI
EXTRA = 8
F32, BF16, I16 = jnp.float32, jnp.bfloat16, jnp.int16


def copies(x, n):
    return jnp.broadcast_to(x[None], (n,) + x.shape)


def spread(x, axis, n):
    return lax.all_to_all(copies(x, n), axis, 0, 0)


def gather_sum(x, axis, n, factor=None):
    got = spread(x, axis, n)
    total = got[0].astype(F32)
    for i in range(1, n):
        total = total + got[i].astype(F32)
    if factor is not None:
        total = total * factor
    return total.astype(BF16)


def shards(counts, cell_totals, gene_totals, test_matrix):
    rows, cols = counts.shape
    scale = 1.0 / math.sqrt(rows * Y_HI * Z * CORE + cols * Y_LO * X)

    low = lax.axis_index("y_hi") == 0
    pieces = jnp.stack([cell_totals >> shift & 2047 for shift in (0, 11, 22)])
    extra = jnp.zeros((EXTRA, cols), I16).at[:3, :rows].set(pieces.astype(I16))
    extra = extra.at[3].set(low.astype(I16))
    mine = jnp.concatenate([counts.astype(I16), extra])
    other = lax.ppermute(mine, "y_hi", [(0, 1), (1, 0)])

    test = spread(test_matrix.T, "z", Z)
    ready, test = lax.optimization_barrier((gene_totals.reshape(8, -1), test))
    totals = spread(jnp.sum(ready, axis=0, keepdims=True), ("y_lo", "x"), Y_LO * X)
    test, totals = lax.optimization_barrier((test, totals))
    test = test.reshape(Z * test_matrix.shape[1], cols)
    total = jnp.sum(totals)
    fraction = gene_totals.astype(F32) / total.astype(F32)

    pair = jnp.stack([jnp.where(low, mine, other), jnp.where(low, other, mine)])
    blocks = lax.all_gather(pair, "core").reshape(BLOCKS, rows + EXTRA, cols)
    pieces = blocks[:, rows : rows + 3, :rows].astype(jnp.int32)
    owned = (pieces[:, 0] + (pieces[:, 1] << 11) + (pieces[:, 2] << 22)).astype(F32)
    expected = owned[:, :, None] * fraction[None, None, :]
    stored = (
        (blocks[:, :rows].astype(F32) - expected)
        * lax.rsqrt(expected * (1.0 + expected * 0.01))
    ).astype(BF16)
    stored = stored.reshape(BLOCKS * rows, cols)

    def cell_side(panel, factor):
        part = lax.dot_general(
            panel, stored, (((1,), (1,)), ((), ())), preferred_element_type=F32
        ).astype(BF16)
        return gather_sum(gather_sum(part, "x", X), "y_lo", Y_LO, factor)

    def gene_side(sketch):
        part = jnp.dot(sketch, stored, preferred_element_type=F32).astype(BF16)
        return gather_sum(part, "z", Z, scale)

    sketch = cell_side(test, 1.0)
    for step in range(ITERS):
        panel = gene_side(sketch)
        sketch = cell_side(panel, scale)
    gene_panel = gene_side(sketch)

    width = sketch.shape[0]
    count = BLOCKS * width
    order = np.arange(count).reshape(CORE, Y_HI, Z, -1).transpose(1, 2, 0, 3).reshape(-1)
    pick = jnp.asarray(np.eye(count)[order], BF16)
    sketch, gene_panel = lax.optimization_barrier((sketch, gene_panel))
    send = jnp.stack(
        [
            jnp.concatenate([sketch[:, i * rows : (i + 1) * rows], gene_panel], axis=1)
            for i in range(BLOCKS)
        ]
    )
    got = lax.all_to_all(send, ("core", "y_hi"), 0, 0)
    got = got.reshape(-1, rows + cols)

    def ordered(block):
        return jnp.dot(pick, block, preferred_element_type=F32).astype(BF16).T

    return (ordered(got[:, :rows]), ordered(got[:, rows:]))


def solution(mesh):
    fine = Mesh(
        np.asarray(mesh.devices).reshape(Y_HI, Z, CORE, Y_LO, X), ("y_hi", "z", "core", "y_lo", "x")
    )
    cell, gene = ("y_hi", "z", "core"), ("y_lo", "x")
    in_specs = (P(cell, gene), P(cell), P(gene), P(gene, cell))
    out_specs = (P(cell, None), P(gene, None))
    return jax.shard_map(shards, mesh=fine, in_specs=in_specs, out_specs=out_specs, check_vma=False)
```

```python
import math

import jax
import jax.numpy as jnp
import numpy as np
from jax import lax
from jax.sharding import Mesh, PartitionSpec as P

ITERS = 3
Y_HI, Z, CORE, Y_LO, X = 2, 8, 2, 4, 4
BLOCKS = CORE * Y_HI
EXTRA = 8
F32, BF16, I16 = jnp.float32, jnp.bfloat16, jnp.int16


def copies(x, n):
    return jnp.broadcast_to(x[None], (n,) + x.shape)


def spread(x, axis, n):
    return lax.all_to_all(copies(x, n), axis, 0, 0)


def gather_sum(x, axis, n, factor=None):
    got = spread(x, axis, n)
    total = got[0].astype(F32)
    for i in range(1, n):
        total = total + got[i].astype(F32)
    if factor is not None:
        total = total * factor
    return total.astype(BF16)


def shards(counts, cell_totals, gene_totals, test_matrix):
    rows, cols = counts.shape
    scale = 1.0 / math.sqrt(rows * Y_HI * Z * CORE + cols * Y_LO * X)

    pieces = jnp.stack([cell_totals >> shift & 2047 for shift in (0, 11, 22)])
    extra = jnp.zeros((EXTRA, cols), I16).at[:3, :rows].set(pieces.astype(I16))
    mine = jnp.concatenate([counts.astype(I16), extra])
    other = lax.ppermute(mine, "y_hi", [(0, 1), (1, 0)])

    test = spread(test_matrix.T, "z", Z)
    ready, test = lax.optimization_barrier((gene_totals.reshape(8, -1), test))
    totals = spread(jnp.sum(ready, axis=0, keepdims=True), ("y_lo", "x"), Y_LO * X)
    test, totals = lax.optimization_barrier((test, totals))
    test = test.reshape(Z * test_matrix.shape[1], cols)
    total = jnp.sum(totals)
    fraction = gene_totals.astype(F32) / total.astype(F32)

    low = lax.axis_index("y_hi") == 0
    pair = jnp.stack([jnp.where(low, mine, other), jnp.where(low, other, mine)])
    blocks = lax.all_gather(pair, "core").reshape(BLOCKS, rows + EXTRA, cols)
    pieces = blocks[:, rows : rows + 3, :rows].astype(jnp.int32)
    owned = (pieces[:, 0] + (pieces[:, 1] << 11) + (pieces[:, 2] << 22)).astype(F32)
    expected = owned[:, :, None] * fraction[None, None, :]
    stored = (
        (blocks[:, :rows].astype(F32) - expected)
        / jnp.sqrt(expected + expected * expected / 100.0)
    ).astype(BF16)
    stored = stored.reshape(BLOCKS * rows, cols)

    def cell_side(panel, factor):
        part = lax.dot_general(
            panel, stored, (((1,), (1,)), ((), ())), preferred_element_type=F32
        ).astype(BF16)
        return gather_sum(gather_sum(part, "y_lo", Y_LO), "x", X, factor)

    def gene_side(sketch):
        part = jnp.dot(sketch, stored, preferred_element_type=F32).astype(BF16)
        return gather_sum(part, "z", Z, scale)

    sketch = cell_side(test, 1.0)
    for step in range(ITERS):
        panel = gene_side(sketch)
        sketch = cell_side(panel, scale)
    gene_panel = gene_side(sketch)

    width = sketch.shape[0]
    count = BLOCKS * width
    order = np.arange(count).reshape(CORE, Y_HI, Z, -1).transpose(1, 2, 0, 3).reshape(-1)
    pick = jnp.asarray(np.eye(count)[order], BF16)
    sketch, gene_panel = lax.optimization_barrier((sketch, gene_panel))
    send = jnp.stack(
        [
            jnp.concatenate([sketch[:, i * rows : (i + 1) * rows], gene_panel], axis=1)
            for i in range(BLOCKS)
        ]
    )
    got = lax.all_to_all(send, ("core", "y_hi"), 0, 0)
    got = got.reshape(-1, rows + cols)

    def ordered(block):
        return jnp.dot(pick, block, preferred_element_type=F32).astype(BF16).T

    return (ordered(got[:, :rows]), ordered(got[:, rows:]))


def solution(mesh):
    fine = Mesh(
        np.asarray(mesh.devices).reshape(Y_HI, Z, CORE, Y_LO, X), ("y_hi", "z", "core", "y_lo", "x")
    )
    cell, gene = ("y_hi", "z", "core"), ("y_lo", "x")
    in_specs = (P(cell, gene), P(cell), P(gene), P(gene, cell))
    out_specs = (P(cell, None), P(gene, None))
    return jax.shard_map(shards, mesh=fine, in_specs=in_specs, out_specs=out_specs, check_vma=False)
```

```python
import math

import jax
import jax.numpy as jnp
import numpy as np
from jax import lax
from jax.experimental import pallas as pl
from jax.experimental.pallas import tpu as pltpu
from jax.sharding import Mesh, PartitionSpec as P

ITERS = 3
Y_HI, Z, CORE, Y_LO, X = 2, 8, 2, 4, 4
BLOCKS, PARTS = CORE * Y_HI, 4
EXTRA = 8
F32, BF16, I16 = jnp.float32, jnp.bfloat16, jnp.int16


def copies(x, n):
    return jnp.broadcast_to(x[None], (n,) + x.shape)


def spread(x, axis, n):
    return lax.all_to_all(copies(x, n), axis, 0, 0)


def gather_sum(x, axis, n, factor=None):
    got = spread(x, axis, n)
    total = got[0].astype(F32)
    for i in range(1, n):
        total = total + got[i].astype(F32)
    if factor is not None:
        total = total * factor
    return total.astype(BF16)


def pack(counts_hbm, totals_hbm, out_ref, counts_ref, totals_ref, sems):
    rows, cols = counts_hbm.shape
    whole = [pltpu.make_async_copy(totals_hbm, totals_ref, sems.at[PARTS])]
    step = rows // PARTS
    for i in range(PARTS):
        part = pl.ds(i * step, step)
        whole.append(pltpu.make_async_copy(counts_hbm.at[part], counts_ref.at[part], sems.at[i]))
    for copy in whole:
        copy.start()
    whole[0].wait()
    shift = jnp.minimum(11 * lax.broadcasted_iota(jnp.int32, (EXTRA, rows), 0), 31)
    pieces = jnp.broadcast_to(totals_ref[...], (EXTRA, rows)) >> shift & 2047
    out_ref[rows:, :rows] = pieces.astype(I16)
    out_ref[rows:, rows:] = jnp.zeros((EXTRA, cols - rows), I16)
    for i in range(PARTS):
        whole[i + 1].wait()
        out_ref[i * step : (i + 1) * step] = counts_ref[i * step : (i + 1) * step].astype(I16)


def shards(counts, cell_totals, gene_totals, test_matrix):
    rows, cols = counts.shape
    scale = 1.0 / math.sqrt(rows * Y_HI * Z * CORE + cols * Y_LO * X)

    mine = pl.pallas_call(
        pack,
        out_shape=jax.ShapeDtypeStruct((rows + EXTRA, cols), I16),
        in_specs=[pl.BlockSpec(memory_space=pltpu.HBM)] * 2,
        out_specs=pl.BlockSpec(memory_space=pltpu.VMEM),
        scratch_shapes=[
            pltpu.VMEM((rows, cols), jnp.int32),
            pltpu.VMEM((1, rows), jnp.int32),
            pltpu.SemaphoreType.DMA((PARTS + 1,)),
        ],
        compiler_params=pltpu.CompilerParams(vmem_limit_bytes=4 << 20),
        cost_estimate=pl.CostEstimate(
            flops=rows * cols, bytes_accessed=6 * rows * cols, transcendentals=0
        ),
    )(
        pltpu.with_memory_space_constraint(counts, pltpu.HBM),
        pltpu.with_memory_space_constraint(cell_totals[None], pltpu.HBM),
    )
    other = lax.ppermute(mine, "y_hi", [(0, 1), (1, 0)])

    test = spread(test_matrix.T, "z", Z)
    ready, test = lax.optimization_barrier((gene_totals.reshape(8, -1), test))
    totals = spread(jnp.sum(ready, axis=0, keepdims=True), ("y_lo", "x"), Y_LO * X)
    test, totals = lax.optimization_barrier((test, totals))
    test = test.reshape(Z * test_matrix.shape[1], cols)
    total = jnp.sum(totals)
    fraction = gene_totals.astype(F32) / total.astype(F32)

    low = lax.axis_index("y_hi") == 0
    pair = jnp.stack([jnp.where(low, mine, other), jnp.where(low, other, mine)])
    blocks = lax.all_gather(pair, "core").reshape(BLOCKS, rows + EXTRA, cols)
    pieces = blocks[:, rows : rows + 3, :rows].astype(jnp.int32)
    owned = (pieces[:, 0] + (pieces[:, 1] << 11) + (pieces[:, 2] << 22)).astype(F32)
    expected = owned[:, :, None] * fraction[None, None, :]
    stored = (
        (blocks[:, :rows].astype(F32) - expected)
        / jnp.sqrt(expected + expected * expected / 100.0)
    ).astype(BF16)
    stored = stored.reshape(BLOCKS * rows, cols)

    def cell_side(panel, factor):
        part = lax.dot_general(
            panel, stored, (((1,), (1,)), ((), ())), preferred_element_type=F32
        ).astype(BF16)
        return gather_sum(gather_sum(part, "x", X), "y_lo", Y_LO, factor)

    def gene_side(sketch):
        part = jnp.dot(sketch, stored, preferred_element_type=F32).astype(BF16)
        return gather_sum(part, "z", Z, scale)

    sketch = cell_side(test, 1.0)
    for step in range(ITERS):
        panel = gene_side(sketch)
        sketch = cell_side(panel, scale)
    gene_panel = gene_side(sketch)

    width = sketch.shape[0]
    count = BLOCKS * width
    order = np.arange(count).reshape(CORE, Y_HI, Z, -1).transpose(1, 2, 0, 3).reshape(-1)
    pick = jnp.asarray(np.eye(count)[order], BF16)
    sketch, gene_panel = lax.optimization_barrier((sketch, gene_panel))
    send = jnp.stack(
        [
            jnp.concatenate([sketch[:, i * rows : (i + 1) * rows], gene_panel], axis=1)
            for i in range(BLOCKS)
        ]
    )
    got = lax.all_to_all(send, ("core", "y_hi"), 0, 0)
    got = got.reshape(-1, rows + cols)

    def ordered(block):
        return jnp.dot(pick, block, preferred_element_type=F32).astype(BF16).T

    return (ordered(got[:, :rows]), ordered(got[:, rows:]))


def solution(mesh):
    fine = Mesh(
        np.asarray(mesh.devices).reshape(Y_HI, Z, CORE, Y_LO, X), ("y_hi", "z", "core", "y_lo", "x")
    )
    cell, gene = ("y_hi", "z", "core"), ("y_lo", "x")
    in_specs = (P(cell, gene), P(cell), P(gene), P(gene, cell))
    out_specs = (P(cell, None), P(gene, None))
    return jax.shard_map(shards, mesh=fine, in_specs=in_specs, out_specs=out_specs, check_vma=False)
```

```python
import math

import jax
import jax.numpy as jnp
import numpy as np
from jax import lax
from jax.experimental import pallas as pl
from jax.experimental.pallas import tpu as pltpu
from jax.sharding import Mesh, PartitionSpec as P

ITERS = 3
Y_HI, Z, CORE, Y_LO, X = 2, 8, 2, 4, 4
BLOCKS, PARTS = CORE * Y_HI, 4
EXTRA = 8
F32, BF16, I16 = jnp.float32, jnp.bfloat16, jnp.int16


def copies(x, n):
    return jnp.broadcast_to(x[None], (n,) + x.shape)


def spread(x, axis, n):
    return lax.all_to_all(copies(x, n), axis, 0, 0)


def gather_sum(x, axis, n, factor=None):
    got = spread(x, axis, n)
    total = got[0].astype(F32)
    for i in range(1, n):
        total = total + got[i].astype(F32)
    if factor is not None:
        total = total * factor
    return total.astype(BF16)


def pack(
    counts_hbm, totals_hbm, genes_hbm, test_hbm, out_ref, genes_ref, test_ref, counts_ref, totals_ref, sems
):
    rows, cols = counts_hbm.shape
    whole = [pltpu.make_async_copy(totals_hbm, totals_ref, sems.at[PARTS])]
    step = rows // PARTS
    for i in range(PARTS):
        part = pl.ds(i * step, step)
        whole.append(pltpu.make_async_copy(counts_hbm.at[part], counts_ref.at[part], sems.at[i]))
    whole.append(pltpu.make_async_copy(genes_hbm, genes_ref, sems.at[PARTS + 1]))
    whole.append(pltpu.make_async_copy(test_hbm, test_ref, sems.at[PARTS + 2]))
    for copy in whole:
        copy.start()
    whole[0].wait()
    shift = jnp.minimum(11 * lax.broadcasted_iota(jnp.int32, (EXTRA, rows), 0), 31)
    pieces = jnp.broadcast_to(totals_ref[...], (EXTRA, rows)) >> shift & 2047
    out_ref[rows:, :rows] = pieces.astype(I16)
    out_ref[rows:, rows:] = jnp.zeros((EXTRA, cols - rows), I16)
    for i in range(PARTS):
        whole[i + 1].wait()
        out_ref[i * step : (i + 1) * step] = counts_ref[i * step : (i + 1) * step].astype(I16)
    whole[PARTS + 1].wait()
    whole[PARTS + 2].wait()


def shards(counts, cell_totals, gene_totals, test_matrix):
    rows, cols = counts.shape
    scale = 1.0 / math.sqrt(rows * Y_HI * Z * CORE + cols * Y_LO * X)

    mine, gene_totals, test = pl.pallas_call(
        pack,
        out_shape=[
            jax.ShapeDtypeStruct((rows + EXTRA, cols), I16),
            jax.ShapeDtypeStruct((8, cols // 8), jnp.int32),
            jax.ShapeDtypeStruct(test_matrix.shape[::-1], BF16),
        ],
        in_specs=[pl.BlockSpec(memory_space=pltpu.HBM)] * 4,
        out_specs=[pl.BlockSpec(memory_space=pltpu.VMEM)] * 3,
        scratch_shapes=[
            pltpu.VMEM((rows, cols), jnp.int32),
            pltpu.VMEM((1, rows), jnp.int32),
            pltpu.SemaphoreType.DMA((PARTS + 3,)),
        ],
        compiler_params=pltpu.CompilerParams(vmem_limit_bytes=4 << 20),
        cost_estimate=pl.CostEstimate(
            flops=rows * cols, bytes_accessed=6 * rows * cols, transcendentals=0
        ),
    )(
        pltpu.with_memory_space_constraint(counts, pltpu.HBM),
        pltpu.with_memory_space_constraint(cell_totals[None], pltpu.HBM),
        pltpu.with_memory_space_constraint(gene_totals.reshape(8, -1), pltpu.HBM),
        pltpu.with_memory_space_constraint(test_matrix.T, pltpu.HBM),
    )
    gene_totals = gene_totals.reshape(-1)
    other = lax.ppermute(mine, "y_hi", [(0, 1), (1, 0)])

    test = spread(test, "z", Z)
    ready, test = lax.optimization_barrier((gene_totals.reshape(8, -1), test))
    totals = spread(jnp.sum(ready, axis=0, keepdims=True), ("y_lo", "x"), Y_LO * X)
    test, totals = lax.optimization_barrier((test, totals))
    test = test.reshape(Z * test_matrix.shape[1], cols)
    total = jnp.sum(totals)
    fraction = gene_totals.astype(F32) / total.astype(F32)

    low = lax.axis_index("y_hi") == 0
    pair = jnp.stack([jnp.where(low, mine, other), jnp.where(low, other, mine)])
    blocks = lax.all_gather(pair, "core").reshape(BLOCKS, rows + EXTRA, cols)
    pieces = blocks[:, rows : rows + 3, :rows].astype(jnp.int32)
    owned = (pieces[:, 0] + (pieces[:, 1] << 11) + (pieces[:, 2] << 22)).astype(F32)
    expected = owned[:, :, None] * fraction[None, None, :]
    stored = (
        (blocks[:, :rows].astype(F32) - expected)
        / jnp.sqrt(expected + expected * expected / 100.0)
    ).astype(BF16)
    stored = stored.reshape(BLOCKS * rows, cols)

    def cell_side(panel, factor):
        part = lax.dot_general(
            panel, stored, (((1,), (1,)), ((), ())), preferred_element_type=F32
        ).astype(BF16)
        return gather_sum(gather_sum(part, "x", X), "y_lo", Y_LO, factor)

    def gene_side(sketch):
        part = jnp.dot(sketch, stored, preferred_element_type=F32).astype(BF16)
        return gather_sum(part, "z", Z, scale)

    sketch = cell_side(test, 1.0)
    for step in range(ITERS):
        panel = gene_side(sketch)
        sketch = cell_side(panel, scale)
    gene_panel = gene_side(sketch)

    width = sketch.shape[0]
    count = BLOCKS * width
    order = np.arange(count).reshape(CORE, Y_HI, Z, -1).transpose(1, 2, 0, 3).reshape(-1)
    pick = jnp.asarray(np.eye(count)[order], BF16)
    sketch, gene_panel = lax.optimization_barrier((sketch, gene_panel))
    send = jnp.stack(
        [
            jnp.concatenate([sketch[:, i * rows : (i + 1) * rows], gene_panel], axis=1)
            for i in range(BLOCKS)
        ]
    )
    got = lax.all_to_all(send, ("core", "y_hi"), 0, 0)
    got = got.reshape(-1, rows + cols)

    def ordered(block):
        return jnp.dot(pick, block, preferred_element_type=F32).astype(BF16).T

    return (ordered(got[:, :rows]), ordered(got[:, rows:]))


def solution(mesh):
    fine = Mesh(
        np.asarray(mesh.devices).reshape(Y_HI, Z, CORE, Y_LO, X), ("y_hi", "z", "core", "y_lo", "x")
    )
    cell, gene = ("y_hi", "z", "core"), ("y_lo", "x")
    in_specs = (P(cell, gene), P(cell), P(gene), P(gene, cell))
    out_specs = (P(cell, None), P(gene, None))
    return jax.shard_map(shards, mesh=fine, in_specs=in_specs, out_specs=out_specs, check_vma=False)
```

```python
import math

import jax
import jax.numpy as jnp
import numpy as np
from jax import lax
from jax.experimental import pallas as pl
from jax.experimental.pallas import tpu as pltpu
from jax.sharding import Mesh, PartitionSpec as P

ITERS = 3
Y_HI, Z, CORE, Y_LO, X = 2, 8, 2, 4, 4
BLOCKS, PARTS = CORE * Y_HI, 4
EXTRA = 8
F32, BF16, I16 = jnp.float32, jnp.bfloat16, jnp.int16


def copies(x, n):
    return jnp.broadcast_to(x[None], (n,) + x.shape)


def spread(x, axis, n):
    return lax.all_to_all(copies(x, n), axis, 0, 0)


def gather_sum(x, axis, n, factor=None):
    got = spread(x, axis, n)
    total = got[0].astype(F32)
    for i in range(1, n):
        total = total + got[i].astype(F32)
    if factor is not None:
        total = total * factor
    return total.astype(BF16)


def pack(
    counts_hbm, totals_hbm, genes_hbm, test_hbm, out_ref, genes_ref, test_ref, counts_ref, totals_ref, sems
):
    rows, cols = counts_hbm.shape
    whole = [pltpu.make_async_copy(totals_hbm, totals_ref, sems.at[PARTS])]
    step = rows // PARTS
    for i in range(PARTS):
        part = pl.ds(i * step, step)
        whole.append(pltpu.make_async_copy(counts_hbm.at[part], counts_ref.at[part], sems.at[i]))
    whole.append(pltpu.make_async_copy(genes_hbm, genes_ref, sems.at[PARTS + 1]))
    whole.append(pltpu.make_async_copy(test_hbm, test_ref, sems.at[PARTS + 2]))
    for copy in whole:
        copy.start()
    whole[0].wait()
    shift = jnp.minimum(11 * lax.broadcasted_iota(jnp.int32, (EXTRA, rows), 0), 31)
    pieces = jnp.broadcast_to(totals_ref[...], (EXTRA, rows)) >> shift & 2047
    out_ref[rows:, :rows] = pieces.astype(I16)
    out_ref[rows:, rows:] = jnp.zeros((EXTRA, cols - rows), I16)
    for i in range(PARTS):
        whole[i + 1].wait()
        out_ref[i * step : (i + 1) * step] = counts_ref[i * step : (i + 1) * step].astype(I16)
    whole[PARTS + 1].wait()
    whole[PARTS + 2].wait()


def place(pick_ref, got_ref, sketch_hbm, panel_hbm, sketch_ref, panel_ref, sems):
    rows = sketch_ref.shape[1]
    panel = jnp.dot(pick_ref[...], got_ref[:, rows:], preferred_element_type=F32)
    panel_ref[...] = panel.astype(BF16)
    first = pltpu.make_async_copy(panel_ref, panel_hbm, sems.at[0])
    first.start()
    sketch = jnp.dot(pick_ref[...], got_ref[:, :rows], preferred_element_type=F32)
    sketch_ref[...] = sketch.astype(BF16)
    second = pltpu.make_async_copy(sketch_ref, sketch_hbm, sems.at[1])
    second.start()
    first.wait()
    second.wait()


def shards(counts, cell_totals, gene_totals, test_matrix):
    rows, cols = counts.shape
    scale = 1.0 / math.sqrt(rows * Y_HI * Z * CORE + cols * Y_LO * X)

    mine, gene_totals, test = pl.pallas_call(
        pack,
        out_shape=[
            jax.ShapeDtypeStruct((rows + EXTRA, cols), I16),
            jax.ShapeDtypeStruct((8, cols // 8), jnp.int32),
            jax.ShapeDtypeStruct(test_matrix.shape[::-1], BF16),
        ],
        in_specs=[pl.BlockSpec(memory_space=pltpu.HBM)] * 4,
        out_specs=[pl.BlockSpec(memory_space=pltpu.VMEM)] * 3,
        scratch_shapes=[
            pltpu.VMEM((rows, cols), jnp.int32),
            pltpu.VMEM((1, rows), jnp.int32),
            pltpu.SemaphoreType.DMA((PARTS + 3,)),
        ],
        compiler_params=pltpu.CompilerParams(vmem_limit_bytes=4 << 20),
        cost_estimate=pl.CostEstimate(
            flops=rows * cols, bytes_accessed=6 * rows * cols, transcendentals=0
        ),
    )(
        pltpu.with_memory_space_constraint(counts, pltpu.HBM),
        pltpu.with_memory_space_constraint(cell_totals[None], pltpu.HBM),
        pltpu.with_memory_space_constraint(gene_totals.reshape(8, -1), pltpu.HBM),
        pltpu.with_memory_space_constraint(test_matrix.T, pltpu.HBM),
    )
    gene_totals = gene_totals.reshape(-1)
    other = lax.ppermute(mine, "y_hi", [(0, 1), (1, 0)])

    test = spread(test, "z", Z)
    ready, test = lax.optimization_barrier((gene_totals.reshape(8, -1), test))
    totals = spread(jnp.sum(ready, axis=0, keepdims=True), ("y_lo", "x"), Y_LO * X)
    test, totals = lax.optimization_barrier((test, totals))
    test = test.reshape(Z * test_matrix.shape[1], cols)
    total = jnp.sum(totals)
    fraction = gene_totals.astype(F32) / total.astype(F32)

    low = lax.axis_index("y_hi") == 0
    pair = jnp.stack([jnp.where(low, mine, other), jnp.where(low, other, mine)])
    blocks = lax.all_gather(pair, "core").reshape(BLOCKS, rows + EXTRA, cols)
    pieces = blocks[:, rows : rows + 3, :rows].astype(jnp.int32)
    owned = (pieces[:, 0] + (pieces[:, 1] << 11) + (pieces[:, 2] << 22)).astype(F32)
    expected = owned[:, :, None] * fraction[None, None, :]
    stored = (
        (blocks[:, :rows].astype(F32) - expected)
        / jnp.sqrt(expected + expected * expected / 100.0)
    ).astype(BF16)
    stored = stored.reshape(BLOCKS * rows, cols)

    def cell_side(panel, factor):
        part = lax.dot_general(
            panel, stored, (((1,), (1,)), ((), ())), preferred_element_type=F32
        ).astype(BF16)
        return gather_sum(gather_sum(part, "x", X), "y_lo", Y_LO, factor)

    def gene_side(sketch):
        part = jnp.dot(sketch, stored, preferred_element_type=F32).astype(BF16)
        return gather_sum(part, "z", Z, scale)

    sketch = cell_side(test, 1.0)
    for step in range(ITERS):
        panel = gene_side(sketch)
        sketch = cell_side(panel, scale)
    gene_panel = gene_side(sketch)

    width = sketch.shape[0]
    count = BLOCKS * width
    order = np.arange(count).reshape(CORE, Y_HI, Z, -1).transpose(1, 2, 0, 3).reshape(-1)
    pick = jnp.asarray(np.eye(count)[order], BF16)
    sketch, gene_panel = lax.optimization_barrier((sketch, gene_panel))
    send = jnp.stack(
        [
            jnp.concatenate([sketch[:, i * rows : (i + 1) * rows], gene_panel], axis=1)
            for i in range(BLOCKS)
        ]
    )
    got = lax.all_to_all(send, ("core", "y_hi"), 0, 0)
    got = got.reshape(-1, rows + cols)

    whole, own = (count, cols), (count, rows)
    sketch, gene_panel = pl.pallas_call(
        place,
        out_shape=[jax.ShapeDtypeStruct(own, BF16), jax.ShapeDtypeStruct(whole, BF16)],
        in_specs=[pl.BlockSpec(memory_space=pltpu.VMEM)] * 2,
        out_specs=[pl.BlockSpec(memory_space=pltpu.HBM)] * 2,
        scratch_shapes=[
            pltpu.VMEM(own, BF16),
            pltpu.VMEM(whole, BF16),
            pltpu.SemaphoreType.DMA((2,)),
        ],
        compiler_params=pltpu.CompilerParams(vmem_limit_bytes=4 << 20),
    )(pick, got)
    return (sketch.T, gene_panel.T)


def solution(mesh):
    fine = Mesh(
        np.asarray(mesh.devices).reshape(Y_HI, Z, CORE, Y_LO, X), ("y_hi", "z", "core", "y_lo", "x")
    )
    cell, gene = ("y_hi", "z", "core"), ("y_lo", "x")
    in_specs = (P(cell, gene), P(cell), P(gene), P(gene, cell))
    out_specs = (P(cell, None), P(gene, None))
    return jax.shard_map(shards, mesh=fine, in_specs=in_specs, out_specs=out_specs, check_vma=False)
```

```python
import math

import jax
import jax.numpy as jnp
import numpy as np
from jax import lax
from jax.experimental import pallas as pl
from jax.experimental.pallas import tpu as pltpu
from jax.sharding import Mesh, PartitionSpec as P

ITERS = 3
Y_HI, Z, CORE, Y_LO, X = 2, 8, 2, 4, 4
BLOCKS, PARTS = CORE * Y_HI, 2
EXTRA = 8
F32, BF16, I16 = jnp.float32, jnp.bfloat16, jnp.int16


def copies(x, n):
    return jnp.broadcast_to(x[None], (n,) + x.shape)


def spread(x, axis, n):
    return lax.all_to_all(copies(x, n), axis, 0, 0)


def gather_sum(x, axis, n, factor=None):
    got = spread(x, axis, n)
    total = got[0].astype(F32)
    for i in range(1, n):
        total = total + got[i].astype(F32)
    if factor is not None:
        total = total * factor
    return total.astype(BF16)


def pack(
    counts_hbm, totals_hbm, genes_hbm, test_hbm, out_ref, genes_ref, test_ref, counts_ref, totals_ref, sems
):
    rows, cols = counts_hbm.shape
    whole = [pltpu.make_async_copy(totals_hbm, totals_ref, sems.at[PARTS])]
    step = rows // PARTS
    for i in range(PARTS):
        part = pl.ds(i * step, step)
        whole.append(pltpu.make_async_copy(counts_hbm.at[part], counts_ref.at[part], sems.at[i]))
    whole.append(pltpu.make_async_copy(genes_hbm, genes_ref, sems.at[PARTS + 1]))
    whole.append(pltpu.make_async_copy(test_hbm, test_ref, sems.at[PARTS + 2]))
    for copy in whole:
        copy.start()
    whole[0].wait()
    shift = jnp.minimum(11 * lax.broadcasted_iota(jnp.int32, (EXTRA, rows), 0), 31)
    pieces = jnp.broadcast_to(totals_ref[...], (EXTRA, rows)) >> shift & 2047
    out_ref[rows:, :rows] = pieces.astype(I16)
    out_ref[rows:, rows:] = jnp.zeros((EXTRA, cols - rows), I16)
    for i in range(PARTS):
        whole[i + 1].wait()
        out_ref[i * step : (i + 1) * step] = counts_ref[i * step : (i + 1) * step].astype(I16)
    whole[PARTS + 1].wait()
    whole[PARTS + 2].wait()


def place(pick_ref, got_ref, sketch_hbm, panel_hbm, sketch_ref, panel_ref, sems):
    rows = sketch_ref.shape[1]
    panel = jnp.dot(pick_ref[...], got_ref[:, rows:], preferred_element_type=F32)
    panel_ref[...] = panel.astype(BF16)
    first = pltpu.make_async_copy(panel_ref, panel_hbm, sems.at[0])
    first.start()
    sketch = jnp.dot(pick_ref[...], got_ref[:, :rows], preferred_element_type=F32)
    sketch_ref[...] = sketch.astype(BF16)
    second = pltpu.make_async_copy(sketch_ref, sketch_hbm, sems.at[1])
    second.start()
    first.wait()
    second.wait()


def shards(counts, cell_totals, gene_totals, test_matrix):
    rows, cols = counts.shape
    scale = 1.0 / math.sqrt(rows * Y_HI * Z * CORE + cols * Y_LO * X)

    mine, gene_totals, test = pl.pallas_call(
        pack,
        out_shape=[
            jax.ShapeDtypeStruct((rows + EXTRA, cols), I16),
            jax.ShapeDtypeStruct((8, cols // 8), jnp.int32),
            jax.ShapeDtypeStruct(test_matrix.shape[::-1], BF16),
        ],
        in_specs=[pl.BlockSpec(memory_space=pltpu.HBM)] * 4,
        out_specs=[pl.BlockSpec(memory_space=pltpu.VMEM)] * 3,
        scratch_shapes=[
            pltpu.VMEM((rows, cols), jnp.int32),
            pltpu.VMEM((1, rows), jnp.int32),
            pltpu.SemaphoreType.DMA((PARTS + 3,)),
        ],
        compiler_params=pltpu.CompilerParams(vmem_limit_bytes=4 << 20),
        cost_estimate=pl.CostEstimate(
            flops=rows * cols, bytes_accessed=6 * rows * cols, transcendentals=0
        ),
    )(
        pltpu.with_memory_space_constraint(counts, pltpu.HBM),
        pltpu.with_memory_space_constraint(cell_totals[None], pltpu.HBM),
        pltpu.with_memory_space_constraint(gene_totals.reshape(8, -1), pltpu.HBM),
        pltpu.with_memory_space_constraint(test_matrix.T, pltpu.HBM),
    )
    gene_totals = gene_totals.reshape(-1)
    other = lax.ppermute(mine, "y_hi", [(0, 1), (1, 0)])

    test = spread(test, "z", Z)
    ready, test = lax.optimization_barrier((gene_totals.reshape(8, -1), test))
    totals = spread(jnp.sum(ready, axis=0, keepdims=True), ("y_lo", "x"), Y_LO * X)
    test, totals = lax.optimization_barrier((test, totals))
    test = test.reshape(Z * test_matrix.shape[1], cols)
    total = jnp.sum(totals)
    fraction = gene_totals.astype(F32) / total.astype(F32)

    low = lax.axis_index("y_hi") == 0
    pair = jnp.stack([jnp.where(low, mine, other), jnp.where(low, other, mine)])
    blocks = lax.all_gather(pair, "core").reshape(BLOCKS, rows + EXTRA, cols)
    pieces = blocks[:, rows : rows + 3, :rows].astype(jnp.int32)
    owned = (pieces[:, 0] + (pieces[:, 1] << 11) + (pieces[:, 2] << 22)).astype(F32)
    expected = owned[:, :, None] * fraction[None, None, :]
    stored = (
        (blocks[:, :rows].astype(F32) - expected)
        / jnp.sqrt(expected + expected * expected / 100.0)
    ).astype(BF16)
    stored = stored.reshape(BLOCKS * rows, cols)

    def cell_side(panel, factor):
        part = lax.dot_general(
            panel, stored, (((1,), (1,)), ((), ())), preferred_element_type=F32
        ).astype(BF16)
        return gather_sum(gather_sum(part, "x", X), "y_lo", Y_LO, factor)

    def gene_side(sketch):
        part = jnp.dot(sketch, stored, preferred_element_type=F32).astype(BF16)
        return gather_sum(part, "z", Z, scale)

    sketch = cell_side(test, 1.0)
    for step in range(ITERS):
        panel = gene_side(sketch)
        sketch = cell_side(panel, scale)
    gene_panel = gene_side(sketch)

    width = sketch.shape[0]
    count = BLOCKS * width
    order = np.arange(count).reshape(CORE, Y_HI, Z, -1).transpose(1, 2, 0, 3).reshape(-1)
    pick = jnp.asarray(np.eye(count)[order], BF16)
    sketch, gene_panel = lax.optimization_barrier((sketch, gene_panel))
    send = jnp.stack(
        [
            jnp.concatenate([sketch[:, i * rows : (i + 1) * rows], gene_panel], axis=1)
            for i in range(BLOCKS)
        ]
    )
    got = lax.all_to_all(send, ("core", "y_hi"), 0, 0)
    got = got.reshape(-1, rows + cols)

    whole, own = (count, cols), (count, rows)
    sketch, gene_panel = pl.pallas_call(
        place,
        out_shape=[jax.ShapeDtypeStruct(own, BF16), jax.ShapeDtypeStruct(whole, BF16)],
        in_specs=[pl.BlockSpec(memory_space=pltpu.VMEM)] * 2,
        out_specs=[pl.BlockSpec(memory_space=pltpu.HBM)] * 2,
        scratch_shapes=[
            pltpu.VMEM(own, BF16),
            pltpu.VMEM(whole, BF16),
            pltpu.SemaphoreType.DMA((2,)),
        ],
        compiler_params=pltpu.CompilerParams(vmem_limit_bytes=4 << 20),
    )(pick, got)
    return (sketch.T, gene_panel.T)


def solution(mesh):
    fine = Mesh(
        np.asarray(mesh.devices).reshape(Y_HI, Z, CORE, Y_LO, X), ("y_hi", "z", "core", "y_lo", "x")
    )
    cell, gene = ("y_hi", "z", "core"), ("y_lo", "x")
    in_specs = (P(cell, gene), P(cell), P(gene), P(gene, cell))
    out_specs = (P(cell, None), P(gene, None))
    return jax.shard_map(shards, mesh=fine, in_specs=in_specs, out_specs=out_specs, check_vma=False)
```
